256 devices in a mesh: row: 16 (over x_lo, y, core), col: 16 (over z, x_hi).
Axes of the slice: x: 4 (x_hi: 2, x_lo: 2; x = x_hi * 2 + x_lo), y: 4, z: 8, core: 2. Of those that a mesh axis runs over, the one named last changes fastest.
Arguments:
- tokens: bfloat16 [1536, 8192], P('row', 'col'), may hold values from -6 to 6
- gate_weight: bfloat16 [8192, 28672], P('col', 'row'), may hold values from -0.0625 to 0.0625
- up_weight: bfloat16 [8192, 28672], P('col', 'row'), may hold values from -0.0625 to 0.0625
- down_weight: bfloat16 [28672, 8192], P('row', 'col'), may hold values from -0.03125 to 0.03125
Outputs:
- mixed: float32 [1536, 8192], P('row', 'col')
The draws below stay inside these ranges and needn't reach their ends.
All inputs are finite; a program needn't handle non-finite values.
Results may differ from the reference program's by a relative error of at most 0.0029.
Values may be sent and summed in bfloat16 or wider, within the bound.
No kernel may reach another device: no remote copies, remote signals or barrier semaphores. Data moves between devices by JAX's collectives and lax.ppermute only.
A program may use at most 128 MiB of HBM per device.

```python
import jax
import jax.numpy as jnp

D = 8192
FF = 28672
TOKENS = 1536


def steps_of(rng, shape, cuts, smallest, top_value):
    level, own = 1.0, jax.random.fold_in(rng, 6)
    for position, shards_of in cuts:
        draws = jnp.exp(jax.random.uniform(jax.random.fold_in(own, position), (shards_of,), jnp.float32, smallest / len(cuts), top_value / len(cuts)))
        level = level * jnp.repeat(draws, shape[position] // shards_of).reshape([-1 if axis == position else 1 for axis in range(len(shape))])
    return level


def centred(stream_key, dims, spread, limit, split=(), dtype=jnp.bfloat16):
    entries = spread * jax.random.normal(stream_key, dims, jnp.float32)
    if split:
        entries = entries * steps_of(stream_key, dims, split, -0.22, 0.18)
    return jnp.clip(entries, -limit, limit).astype(dtype)


def setup_inputs(seed: int = 0) -> dict:
    key_list = jax.random.split(jax.random.key(seed), 5)
    tokens = centred(key_list[0], (TOKENS, D), 1.0, 6.0, ((0, 16), (1, 16)))
    gate_weight = centred(key_list[1], (D, FF), D ** -0.5, 0.0625, ((0, 16), (1, 16)))
    up_weight = centred(key_list[2], (D, FF), D ** -0.5, 0.0625, ((0, 16), (1, 16)))
    down_weight = centred(key_list[3], (FF, D), FF ** -0.5, 0.03125, ((0, 16), (1, 16)))
    return dict(tokens=tokens, gate_weight=gate_weight, up_weight=up_weight, down_weight=down_weight)


def reference(tokens, gate_weight, up_weight, down_weight):
    gate = jnp.dot(tokens, gate_weight, preferred_element_type=jnp.float32)
    up = jnp.dot(tokens, up_weight, preferred_element_type=jnp.float32)
    hidden = (jax.nn.silu(gate) * up).astype(jnp.bfloat16)
    return jnp.dot(hidden, down_weight, preferred_element_type=jnp.float32)
```

```python
import itertools

import jax
import jax.numpy as jnp
from jax import lax
from jax.sharding import Mesh, PartitionSpec as P

AXES = ("xl", "y", "c", "z", "xh")
SIZES = (2, 4, 2, 8, 2)
CHUNKS = 2
EARLY, LATE = (0, 1, 7, 2), (6, 3, 5, 4)
F32, BF16 = jnp.float32, jnp.bfloat16


def send(value, move):
    flat = lambda at: sum(i * k for i, k in zip(at, (128, 32, 16, 2, 1)))
    pairs = []
    for at in itertools.product(*map(range, SIZES)):
        to = move(*at)
        if to is not None:
            pairs.append((flat(at), flat(tuple(i % n for i, n in zip(to, SIZES)))))
    return lax.ppermute(value, AXES, pairs)


def along_z(value, step):
    return send(value, lambda xl, y, c, z, xh: (xl, y, c, z + step, xh))


def along_y(value, step):
    return send(value, lambda xl, y, c, z, xh: (xl, y + step, c, z, xh))


def swap_xl(value):
    return send(value, lambda xl, y, c, z, xh: (1 - xl, y, c, z, xh))


def swap_xh(value):
    return send(value, lambda xl, y, c, z, xh: (xl, y, c, z, 1 - xh))


def swap_core(value):
    return send(value, lambda xl, y, c, z, xh: (xl, y, 1 - c, z, xh))


def rows_dot(a, b):
    return lax.dot_general(a, b, (((1,), (1,)), ((), ())), preferred_element_type=F32)


def columns_dot(a, b):
    return lax.dot_general(a, b, (((0,), (0,)), ((), ())), preferred_element_type=F32)


def shards(tokens, gate_weight, up_weight, down_weight):
    xl, y, c, z, xh = (lax.axis_index(a) for a in AXES)
    nz = SIZES[3]

    token = {0: tokens}
    for s in (1, 7, 2, 6, 3, 5, 4):
        token[s] = along_z(tokens, s)

    units = gate_weight.shape[1] // nz
    sliced = [
        lax.optimization_barrier(w.T).reshape(nz, units, -1) for w in (gate_weight, up_weight)
    ]
    weight = {}
    for s in EARLY + LATE:
        to = lax.rem(z + s, nz)
        piece = jnp.concatenate([lax.dynamic_index_in_dim(w, to, 0, False) for w in sliced])
        weight[s] = along_z(piece, s) if s else piece
    own = [jnp.concatenate([weight[s] for s in half], 1) for half in (EARLY, LATE)]
    other = [swap_core(w) for w in own]

    moved = send(
        down_weight,
        lambda xl, y, c, z, xh: (xl, y, 1 - c, z, 1 - xh) if c != xh else None,
    )
    mine = jnp.where(c == xh, down_weight, moved)
    theirs = swap_core(mine)
    down = []
    for d in (0, 1):
        w = jnp.where(c == d, mine, theirs).reshape(nz, units, -1)
        order = lax.rem(z - jnp.arange(nz) + nz, nz)
        down.append(jnp.concatenate([lax.dynamic_index_in_dim(w, order[s], 0, False) for s in range(nz)]))

    rows = tokens.shape[0] // CHUNKS
    outs = []
    for i in range(CHUNKS):
        halves = []
        block = jnp.concatenate(
            [token[s][i * rows : (i + 1) * rows] for s in EARLY + LATE], 1
        )
        far = swap_xl(block)
        block = jnp.where(
            xl == 0, jnp.concatenate([block, far]), jnp.concatenate([far, block])
        )
        before, after = along_y(block, 1), along_y(block, -1)
        half = block.shape[0] // 2
        across = jnp.concatenate([along_y(before[:half], 1), along_y(after[half:], -1)])
        ring = jnp.concatenate([block, after, across, before])
        ring = jnp.concatenate([ring, ring])
        ring = lax.dynamic_slice_in_dim(ring, lax.rem(4 - y, 4) * block.shape[0], 4 * block.shape[0], 0)
        cut = ring.shape[1] // 2
        t = (ring[:, :cut], ring[:, cut:])

        here = rows_dot(own[0], t[0]) + rows_dot(own[1], t[1])
        there = rows_dot(other[0], t[0]) + rows_dot(other[1], t[1])
        keep = jnp.where(c == xh, here, there)
        give = jnp.where(c == xh, there, here)
        total = keep + swap_xh(give)
        hidden = (jax.nn.silu(total[:units]) * total[units:]).astype(BF16)

        part = {0: hidden}
        forward = backward = hidden
        for s in (1, 2, 3):
            part[s] = forward = along_z(forward, 1)
            part[nz - s] = backward = along_z(backward, -1)
        half = units // 2
        part[4] = jnp.concatenate([along_z(forward[:half], 1), along_z(backward[half:], -1)])
        gathered = jnp.concatenate([part[s] for s in range(nz)])
        out = jnp.concatenate([columns_dot(gathered, w).astype(BF16) for w in down])
        out = out.reshape(16, rows, -1)
        got = lax.all_to_all(out, ("xh", "y", "xl"), 0, 0, tiled=True)
        outs.append(jnp.sum(got.astype(F32), 0))
    return jnp.concatenate(outs)


def solution(mesh):
    split = Mesh(mesh.devices.reshape(SIZES), AXES)
    row, col = ("xl", "y", "c"), ("z", "xh")
    return jax.shard_map(
        shards,
        mesh=split,
        in_specs=(P(row, col), P(col, row), P(col, row), P(row, col)),
        out_specs=P(row, col),
        check_vma=False,
    )
```

```python
import functools
import itertools

import jax
import jax.numpy as jnp
from jax import lax
from jax.experimental import pallas as pl
from jax.experimental.pallas import tpu as pltpu
from jax.sharding import Mesh, PartitionSpec as P

AXES = ("xl", "y", "c", "z", "xh")
SIZES = (2, 4, 2, 8, 2)
CHUNKS = 2
F32, BF16 = jnp.float32, jnp.bfloat16
SCALARS = pl.BlockSpec(memory_space=pltpu.SMEM)
WHOLE = pl.BlockSpec(memory_space=pltpu.VMEM)


def send(value, move):
    flat = lambda at: sum(i * k for i, k in zip(at, (128, 32, 16, 2, 1)))
    pairs = []
    for at in itertools.product(*map(range, SIZES)):
        to = move(*at)
        if to is not None:
            pairs.append((flat(at), flat(tuple(i % n for i, n in zip(to, SIZES)))))
    return lax.ppermute(value, AXES, pairs)


def along_z(value, step):
    return send(value, lambda xl, y, c, z, xh: (xl, y, c, z + step, xh))


def along_y(value, step):
    return send(value, lambda xl, y, c, z, xh: (xl, y + step, c, z, xh))


def swap_xl(value):
    return send(value, lambda xl, y, c, z, xh: (1 - xl, y, c, z, xh))


def swap_xh(value):
    return send(value, lambda xl, y, c, z, xh: (xl, y, c, z, 1 - xh))


def swap_core(value):
    return send(value, lambda xl, y, c, z, xh: (xl, y, 1 - c, z, xh))


def together(*values):
    return lax.optimization_barrier(values)


def cost(flops, *arrays):
    size = sum(a.size * a.dtype.itemsize for a in arrays)
    return pl.CostEstimate(flops=flops, bytes_accessed=size, transcendentals=0)


def slice_units(gate, up, nz):
    depth, width = gate.shape
    units = width // nz
    step = 128

    def body(g_ref, u_ref, o_ref):
        o_ref[:, :units] = g_ref[...].T.reshape(nz, units, step)
        o_ref[:, units:] = u_ref[...].T.reshape(nz, units, step)

    out = jax.ShapeDtypeStruct((nz, 2 * units, depth), gate.dtype)
    return pl.pallas_call(
        body,
        grid=(depth // step,),
        in_specs=[pl.BlockSpec((step, width), lambda k: (k, 0))] * 2,
        out_specs=pl.BlockSpec((nz, 2 * units, step), lambda k: (0, 0, k)),
        out_shape=out,
        cost_estimate=cost(0, gate, up, out),
        name="slice_units",
    )(gate, up)


def project(place, weight, pieces, here=None):
    near, far, before, after, across_0, across_1 = pieces
    nz, units, depth = weight.shape
    rows = near.shape[1]
    last = here is not None

    def body(place_ref, w_ref, near_ref, far_ref, before_ref, after_ref, a0_ref, a1_ref, *rest):
        here_ref = rest[0] if last else None
        outs, (t_ref, acc_ref) = rest[last:-2], rest[-2:]
        xl, y = place_ref[0], place_ref[1]
        found = (
            (0, 0, near_ref[0]), (0, 1, far_ref[0]),
            (1, 0, after_ref[0, 0]), (1, 1, after_ref[1, 0]),
            (2, 0, a0_ref[0]), (2, 1, a1_ref[0]),
            (3, 0, before_ref[0, 0]), (3, 1, before_ref[1, 0]),
        )
        for dy, dx, piece in found:
            at = ((y + dy) % 4) * 2 + (xl + dx) % 2
            t_ref[pl.ds(pl.multiple_of(at * rows, rows), rows)] = piece
        k = pl.program_id(0)
        term = lax.dot_general(
            w_ref[0], t_ref[...], (((1,), (1,)), ((), ())), preferred_element_type=F32
        )

        @pl.when(k == 0)
        def _():
            acc_ref[...] = term

        @pl.when(k > 0)
        def _():
            acc_ref[...] += term

        @pl.when(k == nz - 1)
        def _():
            if last:
                same = place_ref[2] == place_ref[4]
                outs[0][...] = jnp.where(same, here_ref[...], acc_ref[...])
                outs[1][...] = jnp.where(same, acc_ref[...], here_ref[...])
            else:
                outs[0][...] = acc_ref[...]

    one = pl.BlockSpec((1, rows, depth), lambda k: (k, 0, 0))
    two = pl.BlockSpec((2, 1, rows, depth), lambda k: (0, k, 0, 0))
    full = pl.BlockSpec((units, 8 * rows), lambda k: (0, 0))
    out = jax.ShapeDtypeStruct((units, 8 * rows), F32)
    args = (weight, *pieces) + ((here,) if last else ())
    return pl.pallas_call(
        body,
        grid=(nz,),
        in_specs=[SCALARS, pl.BlockSpec((1, units, depth), lambda k: (k, 0, 0)), one, one, two, two, one, one]
        + [full] * last,
        out_specs=[full] * (1 + last),
        out_shape=[out] * (1 + last),
        scratch_shapes=[pltpu.VMEM((8 * rows, depth), BF16), pltpu.VMEM((units, 8 * rows), F32)],
        cost_estimate=cost(2 * nz * units * depth * 8 * rows, *args),
        name="project_last" if last else "project",
    )(place, *args)


def activate(keep, got):
    units, rows = keep.shape[0] // 2, keep.shape[1]

    def body(keep_ref, got_ref, o_ref):
        gate = keep_ref[:units] + got_ref[:units]
        up = keep_ref[units:] + got_ref[units:]
        o_ref[...] = (gate / (1 + jnp.exp(-gate)) * up).astype(o_ref.dtype)

    return pl.pallas_call(
        body,
        in_specs=[WHOLE] * 2,
        out_specs=WHOLE,
        out_shape=jax.ShapeDtypeStruct((units, rows), BF16),
        cost_estimate=cost(0, keep, got),
        name="activate",
    )(keep, got)


def mix(place, parts, mine, theirs):
    units, rows = parts[0].shape
    width = mine.shape[1]
    nz = SIZES[3]

    def body(place_ref, mine_ref, theirs_ref, *rest):
        part_refs, (o_ref, h_ref) = rest[:-2], rest[-2:]
        c, z = place_ref[2], place_ref[3]
        at = 0
        for s in range(nz):
            slot = pl.multiple_of(((z + nz - s) % nz) * units, units)
            if s == nz // 2:
                low, high = part_refs[s], part_refs[s + 1]
                h_ref[pl.ds(slot, units // 2)] = low[...]
                h_ref[pl.ds(pl.multiple_of(slot + units // 2, units // 2), units // 2)] = high[...]
            else:
                h_ref[pl.ds(slot, units)] = part_refs[s + (s > nz // 2)][...]
        for side, w_ref in ((c, mine_ref), (1 - c, theirs_ref)):
            o_ref[side] = lax.dot_general(
                h_ref[...], w_ref[...], (((0,), (0,)), ((), ())), preferred_element_type=F32
            ).astype(o_ref.dtype)

    return pl.pallas_call(
        body,
        in_specs=[SCALARS] + [WHOLE] * (2 + len(parts)),
        out_specs=WHOLE,
        out_shape=jax.ShapeDtypeStruct((2, rows, width), BF16),
        scratch_shapes=[pltpu.VMEM((nz * units, rows), BF16)],
        cost_estimate=cost(4 * nz * units * rows * width, mine, theirs, *parts),
        name="mix",
    )(place, mine, theirs, *parts)


def shards(tokens, gate_weight, up_weight, down_weight):
    xl, y, c, z, xh = (lax.axis_index(a) for a in AXES)
    place = jnp.stack([xl, y, c, z, xh]).astype(jnp.int32)
    nz = SIZES[3]
    rows = tokens.shape[0] // CHUNKS

    token = jnp.broadcast_to(tokens[None], (nz, *tokens.shape))
    token = lax.all_to_all(token, "z", 0, 0, tiled=True)

    sliced, token = together(slice_units(gate_weight, up_weight, nz), token)
    weight = lax.all_to_all(sliced, "z", 0, 0, tiled=True)

    nears = [token[:, i * rows : (i + 1) * rows] for i in range(CHUNKS)]
    fars = [swap_xl(near) for near in nears]
    chunks = []
    for near, far in zip(nears, fars):
        pair = jnp.stack([near, far])
        before, after = along_y(pair, 1), along_y(pair, -1)
        across_0, across_1 = along_y(before[0], 1), along_y(after[1], -1)
        chunks.append((near, far, before, after, across_0, across_1))

    down_weight, *fars = together(down_weight, *fars)
    moved = send(
        down_weight,
        lambda xl, y, c, z, xh: (xl, y, 1 - c, z, 1 - xh) if c != xh else None,
    )
    mine = jnp.where(c == xh, down_weight, moved)
    theirs = swap_core(mine)
    weight, mine, theirs, chunks = together(weight, mine, theirs, chunks)
    other = swap_core(weight)

    heres = [project(place, weight, pieces)[0] for pieces in chunks]
    other, heres = together(other, heres)
    sums = [project(place, other, pieces, here) for pieces, here in zip(chunks, heres)]
    gots = [swap_xh(give) for _, give in sums]

    rings, outs = [], []
    ends = 2 * (CHUNKS - 1) + nz // 2
    for step in range(ends + 1):
        for i in range(CHUNKS):
            at = step - 2 * i
            if at == 0:
                hidden = activate(sums[i][0], gots[i])
                rings.append({0: hidden, "up": hidden, "down": hidden})
            if 0 <= at < nz // 2:
                ring = rings[i]
                up, down = ring["up"], ring["down"]
                if at == nz // 2 - 1:
                    half = up.shape[0] // 2
                    up, down = up[:half], down[half:]
                up, down = along_z(up, 1), along_z(down, -1)
                ring.update({"up": up, "down": down, at + 1: up, -at - 1: down})
            if at == nz // 2:
                ring = rings[i]
                parts = [ring[s] for s in (0, 1, 2, 3, 4, -4, -3, -2, -1)]
                out = mix(place, parts, mine, theirs).reshape(16, rows, -1)
                got = lax.all_to_all(out, ("xh", "y", "xl"), 0, 0, tiled=True)
                outs.append(jnp.sum(got.astype(F32), 0))
        live = [i for i in range(CHUNKS) if 0 <= step - 2 * i < nz // 2]
        if len(live) > 1 or step == 1:
            held = [(rings[i]["up"], rings[i]["down"]) for i in live]
            if step == 1:
                held, gots[1] = together(held, gots[1])
            else:
                held = together(*held)
            for i, (up, down) in zip(live, held):
                rings[i].update({"up": up, "down": down})
    return jnp.concatenate(outs)


def solution(mesh):
    split = Mesh(mesh.devices.reshape(SIZES), AXES)
    row, col = ("xl", "y", "c"), ("z", "xh")
    return jax.shard_map(
        shards,
        mesh=split,
        in_specs=(P(row, col), P(col, row), P(col, row), P(row, col)),
        out_specs=P(row, col),
        check_vma=False,
    )
```

```python
import functools
import itertools

import jax
import jax.numpy as jnp
from jax import lax
from jax.experimental import pallas as pl
from jax.experimental.pallas import tpu as pltpu
from jax.sharding import Mesh, PartitionSpec as P

AXES = ("xl", "y", "c", "z", "xh")
SIZES = (2, 4, 2, 8, 2)
CHUNKS = 2
FIRST = 160
TOGETHER = 2
F32, BF16 = jnp.float32, jnp.bfloat16
SCALARS = pl.BlockSpec(memory_space=pltpu.SMEM)
WHOLE = pl.BlockSpec(memory_space=pltpu.VMEM)


def send(value, move):
    flat = lambda at: sum(i * k for i, k in zip(at, (128, 32, 16, 2, 1)))
    pairs = []
    for at in itertools.product(*map(range, SIZES)):
        to = move(*at)
        if to is not None:
            pairs.append((flat(at), flat(tuple(i % n for i, n in zip(to, SIZES)))))
    return lax.ppermute(value, AXES, pairs)


def along_z(value, step):
    return send(value, lambda xl, y, c, z, xh: (xl, y, c, z + step, xh))


def along_y(value, step):
    return send(value, lambda xl, y, c, z, xh: (xl, y + step, c, z, xh))


def swap_xl(value):
    return send(value, lambda xl, y, c, z, xh: (1 - xl, y, c, z, xh))


def swap_xh(value):
    return send(value, lambda xl, y, c, z, xh: (xl, y, c, z, 1 - xh))


def swap_core(value):
    return send(value, lambda xl, y, c, z, xh: (xl, y, 1 - c, z, xh))


def together(*values):
    return lax.optimization_barrier(values)


def cost(flops, *arrays):
    size = sum(a.size * a.dtype.itemsize for a in arrays)
    return pl.CostEstimate(flops=flops // 64, bytes_accessed=size // 64, transcendentals=0)


def regroup(place, parts):
    nz = SIZES[3]

    def body(place_ref, *rest):
        z = place_ref[3]
        for s, part_ref in enumerate(rest[:nz]):
            rest[nz][(z + nz - s) % nz] = part_ref[...]

    return pl.pallas_call(
        body,
        in_specs=[SCALARS] + [WHOLE] * nz,
        out_specs=WHOLE,
        out_shape=jax.ShapeDtypeStruct((nz, *parts[0].shape), BF16),
        cost_estimate=cost(0, *parts, *parts),
        name="regroup",
    )(place, *parts)


def slice_units(gate, up, nz):
    depth, width = gate.shape
    units = width // nz
    step = 256
    cuts = ((0, FIRST), (FIRST, units))

    def body(g_ref, u_ref, *o_refs):
        for w_ref, at in ((g_ref, 0), (u_ref, 1)):
            w = w_ref[...].T.reshape(nz, units, step)
            for (lo, hi), o_ref in zip(cuts, o_refs):
                o_ref[:, at * (hi - lo) : (at + 1) * (hi - lo)] = w[:, lo:hi]

    outs = [jax.ShapeDtypeStruct((nz, 2 * (hi - lo), depth), gate.dtype) for lo, hi in cuts]
    return pl.pallas_call(
        body,
        grid=(depth // step,),
        in_specs=[pl.BlockSpec((step, width), lambda k: (k, 0))] * 2,
        out_specs=[pl.BlockSpec((*o.shape[:2], step), lambda k: (0, 0, k)) for o in outs],
        out_shape=outs,
        cost_estimate=cost(0, gate, up, *outs),
        name="slice_units",
    )(gate, up)


def project(place, weight, pieces, here=None):
    nz, units, depth = weight.shape
    rows = pieces[0].shape[1] // CHUNKS
    width = 8 * rows * CHUNKS
    last = here is not None

    def body(place_ref, w_ref, *rest):
        piece_refs, rest = rest[:8], rest[8:]
        here_ref = rest[0] if last else None
        outs, (t_ref, acc_ref) = rest[last:-2], rest[-2:]
        xl, y = place_ref[0], place_ref[1]
        k = pl.program_id(0)
        term = None
        for j in range(TOGETHER):
            for n, piece_ref in enumerate(piece_refs):
                at = ((y + n // 2) % 4) * 2 + (xl + n % 2) % 2
                for i in range(CHUNKS):
                    to = pl.multiple_of((8 * i + at) * rows, rows)
                    t_ref[j, pl.ds(to, rows)] = piece_ref[j, i * rows : (i + 1) * rows]
            product = lax.dot_general(
                w_ref[j], t_ref[j], (((1,), (1,)), ((), ())), preferred_element_type=F32
            )
            term = product if term is None else term + product

        @pl.when(k == 0)
        def _():
            acc_ref[...] = term

        @pl.when(k > 0)
        def _():
            acc_ref[...] += term

        @pl.when(k == nz // TOGETHER - 1)
        def _():
            if last:
                same = place_ref[2] == place_ref[4]
                outs[0][...] = jnp.where(same, here_ref[...], acc_ref[...])
                outs[1][...] = jnp.where(same, acc_ref[...], here_ref[...])
            else:
                outs[0][...] = acc_ref[...]

    full = pl.BlockSpec((units, width), lambda k: (0, 0))
    out = jax.ShapeDtypeStruct((units, width), F32)
    args = (weight, *pieces) + ((here,) if last else ())
    return pl.pallas_call(
        body,
        grid=(nz // TOGETHER,),
        in_specs=[SCALARS, pl.BlockSpec((TOGETHER, units, depth), lambda k: (k, 0, 0))]
        + [pl.BlockSpec((TOGETHER, CHUNKS * rows, depth), lambda k: (k, 0, 0))] * 8
        + [full] * last,
        out_specs=[full] * (1 + last),
        out_shape=[out] * (1 + last),
        scratch_shapes=[pltpu.VMEM((TOGETHER, width, depth), BF16), pltpu.VMEM((units, width), F32)],
        cost_estimate=cost(2 * nz * units * depth * width, *args),
        name="project_last" if last else "project",
    )(place, *args)


def activate(keep, got):
    units, rows = keep.shape[0] // 2, keep.shape[1]

    def body(keep_ref, got_ref, o_ref):
        gate = keep_ref[:units] + got_ref[:units]
        up = keep_ref[units:] + got_ref[units:]
        o_ref[...] = (gate / (1 + jnp.exp(-gate)) * up).astype(o_ref.dtype)

    return pl.pallas_call(
        body,
        in_specs=[WHOLE] * 2,
        out_specs=WHOLE,
        out_shape=jax.ShapeDtypeStruct((units, rows), BF16),
        cost_estimate=cost(0, keep, got),
        name="activate",
    )(keep, got)


def mix(place, chunk, rings, mine, theirs):
    nz = SIZES[3]
    sizes = [ring[0].shape[0] for ring in rings]
    units, rows = sum(sizes), rings[0][0].shape[1] // CHUNKS
    width = mine.shape[1]
    order = (0, 1, 2, 3, 4, -4, -3, -2, -1)
    parts = [ring[s] for ring in rings for s in order]

    def body(place_ref, mine_ref, theirs_ref, *rest):
        part_refs, (o_ref, h_ref) = list(rest[:-2]), rest[-2:]
        c, z = place_ref[2], place_ref[3]
        first = 0
        for size in sizes:
            for s in order:
                length = size // 2 if abs(s) == nz // 2 else size
                at = ((z - s + nz) % nz) * units + first + (length if s == -nz // 2 else 0)
                h_ref[pl.ds(pl.multiple_of(at, 16), length)] = part_refs.pop(0)[...]
            first += size
        for side, w_ref in ((c, mine_ref), (1 - c, theirs_ref)):
            o_ref[side] = lax.dot_general(
                h_ref[...], w_ref[...], (((0,), (0,)), ((), ())), preferred_element_type=F32
            ).astype(o_ref.dtype)

    return pl.pallas_call(
        body,
        grid=(1,),
        in_specs=[SCALARS]
        + [pl.BlockSpec(mine.shape, lambda k: (0, 0))] * 2
        + [pl.BlockSpec((p.shape[0], rows), lambda k: (0, chunk)) for p in parts],
        out_specs=pl.BlockSpec((2, rows, width), lambda k: (0, 0, 0)),
        out_shape=jax.ShapeDtypeStruct((2, rows, width), BF16),
        scratch_shapes=[pltpu.VMEM((nz * units, rows), BF16)],
        cost_estimate=cost(4 * nz * units * rows * width, mine, theirs, *parts),
        name="mix",
    )(place, mine, theirs, *parts)


def shards(tokens, gate_weight, up_weight, down_weight):
    xl, y, c, z, xh = (lax.axis_index(a) for a in AXES)
    place = jnp.stack([xl, y, c, z, xh]).astype(jnp.int32)
    nz = SIZES[3]
    rows = tokens.shape[0] // CHUNKS

    around = {0: tokens}
    for s in (1, -1, 2, -2, 4):
        around[s] = along_z(tokens, s)
    around[3], around[-3] = along_z(around[2], 1), along_z(around[-2], -1)
    sliced = slice_units(gate_weight, up_weight, nz)
    ready, *around = together(sliced[0], *(around[s] for s in (0, 1, 2, 3, 4, -3, -2, -1)))
    weights = [lax.all_to_all(ready, "z", 0, 0, tiled=True)]

    near = regroup(place, around)
    far = swap_xl(near)
    near_before, near_after = along_y(near, 1), along_y(near, -1)
    far_before, far_after = along_y(far, 1), along_y(far, -1)
    ready, weights[0], near_before, near_after, far_before, far_after = together(
        sliced[1], weights[0], near_before, near_after, far_before, far_after
    )
    weights.append(lax.all_to_all(ready, "z", 0, 0, tiled=True))
    near_across, far_across = along_y(near_before, 1), along_y(far_after, -1)
    pieces = (near, far, near_after, far_after, near_across, far_across, near_before, far_before)

    def sums(weight):
        other = swap_core(weight)
        here = project(place, weight, pieces)[0]
        return project(place, other, pieces, here)

    keep, give = sums(weights[0])
    got = swap_xh(give)
    hiddens = [activate(keep, got)]

    down_weight, _ = together(down_weight, far)
    moved = send(
        down_weight,
        lambda xl, y, c, z, xh: (xl, y, 1 - c, z, 1 - xh) if c != xh else None,
    )
    moved, weights[1], _ = together(moved, weights[1], give)
    mine = jnp.where(c == xh, down_weight, moved)
    keep, give = sums(weights[1])
    hiddens.append(activate(keep, swap_xh(give)))
    mine, _ = together(mine, give)
    theirs = swap_core(mine)

    rings = []
    for hidden in hiddens:
        ring, up, down = {0: hidden}, hidden, hidden
        for at in range(nz // 2):
            if at == nz // 2 - 1:
                half = up.shape[0] // 2
                up, down = up[:half], down[half:]
            up, down = along_z(up, 1), along_z(down, -1)
            ring.update({at + 1: up, -at - 1: down})
        rings.append(ring)

    outs = []
    for i in range(CHUNKS):
        out = mix(place, i, rings, mine, theirs).reshape(16, rows, -1)
        got = lax.all_to_all(out, ("xh", "y", "xl"), 0, 0, tiled=True)
        outs.append(jnp.sum(got.astype(F32), 0))
    return jnp.concatenate(outs)


def solution(mesh):
    split = Mesh(mesh.devices.reshape(SIZES), AXES)
    row, col = ("xl", "y", "c"), ("z", "xh")
    return jax.shard_map(
        shards,
        mesh=split,
        in_specs=(P(row, col), P(col, row), P(col, row), P(row, col)),
        out_specs=P(row, col),
        check_vma=False,
    )
```

```python
import functools
import itertools

import jax
import jax.numpy as jnp
from jax import lax
from jax.experimental import pallas as pl
from jax.experimental.pallas import tpu as pltpu
from jax.sharding import Mesh, PartitionSpec as P

AXES = ("xl", "y", "c", "z", "xh")
SIZES = (2, 4, 2, 8, 2)
CHUNKS = 2
FIRST = 160
TOGETHER = 2
F32, BF16 = jnp.float32, jnp.bfloat16
SCALARS = pl.BlockSpec(memory_space=pltpu.SMEM)
WHOLE = pl.BlockSpec(memory_space=pltpu.VMEM)


def send(value, move):
    flat = lambda at: sum(i * k for i, k in zip(at, (128, 32, 16, 2, 1)))
    pairs = []
    for at in itertools.product(*map(range, SIZES)):
        to = move(*at)
        if to is not None:
            pairs.append((flat(at), flat(tuple(i % n for i, n in zip(to, SIZES)))))
    return lax.ppermute(value, AXES, pairs)


def along_z(value, step):
    return send(value, lambda xl, y, c, z, xh: (xl, y, c, z + step, xh))


def along_y(value, step):
    return send(value, lambda xl, y, c, z, xh: (xl, y + step, c, z, xh))


def swap_xl(value):
    return send(value, lambda xl, y, c, z, xh: (1 - xl, y, c, z, xh))


def swap_xh(value):
    return send(value, lambda xl, y, c, z, xh: (xl, y, c, z, 1 - xh))


def swap_core(value):
    return send(value, lambda xl, y, c, z, xh: (xl, y, 1 - c, z, xh))


def together(*values):
    return lax.optimization_barrier(values)


def room(mib):
    return pltpu.CompilerParams(vmem_limit_bytes=mib << 20)


def cost(flops, *arrays):
    size = sum(a.size * a.dtype.itemsize for a in arrays)
    return pl.CostEstimate(flops=flops // 64, bytes_accessed=size // 64, transcendentals=0)


def regroup(place, parts):
    nz = SIZES[3]

    def body(place_ref, *rest):
        z = place_ref[3]
        for s, part_ref in enumerate(rest[:nz]):
            rest[nz][(z + nz - s) % nz] = part_ref[...]

    return pl.pallas_call(
        body,
        in_specs=[SCALARS] + [WHOLE] * nz,
        out_specs=WHOLE,
        out_shape=jax.ShapeDtypeStruct((nz, *parts[0].shape), BF16),
        cost_estimate=cost(0, *parts, *parts),
        name="regroup",
        compiler_params=room(4),
    )(place, *parts)


def slice_units(gate, up, nz):
    depth, width = gate.shape
    units = width // nz
    step = 256
    cuts = ((0, FIRST), (FIRST, units))

    def body(g_ref, u_ref, *o_refs):
        for w_ref, at in ((g_ref, 0), (u_ref, 1)):
            w = w_ref[...].T.reshape(nz, units, step)
            for (lo, hi), o_ref in zip(cuts, o_refs):
                o_ref[:, at * (hi - lo) : (at + 1) * (hi - lo)] = w[:, lo:hi]

    outs = [jax.ShapeDtypeStruct((nz, 2 * (hi - lo), depth), gate.dtype) for lo, hi in cuts]
    return pl.pallas_call(
        body,
        grid=(depth // step,),
        in_specs=[pl.BlockSpec((step, width), lambda k: (k, 0))] * 2,
        out_specs=[pl.BlockSpec((*o.shape[:2], step), lambda k: (0, 0, k)) for o in outs],
        out_shape=outs,
        cost_estimate=cost(0, gate, up, *outs),
        name="slice_units",
        compiler_params=room(12),
    )(gate, up)


def project(place, own, other, pieces):
    nz, units, depth = own.shape
    rows = pieces[0].shape[1] // CHUNKS
    width = 8 * rows * CHUNKS
    groups = nz // TOGETHER

    def body(place_ref, own_ref, other_ref, *rest):
        piece_refs, (keep_ref, give_ref, t_ref, w_ref, acc_ref, sems) = rest[:8], rest[8:]
        xl, y = place_ref[0], place_ref[1]

        def copies(g):
            zs = pl.ds(g * TOGETHER, TOGETHER)
            pairs = [(own_ref.at[zs], w_ref.at[0, zs]), (other_ref.at[zs], w_ref.at[1, zs])]
            for n, piece_ref in enumerate(piece_refs):
                at = ((y + n // 2) % 4) * 2 + (xl + n % 2) % 2
                for i in range(CHUNKS):
                    to = pl.multiple_of((8 * i + at) * rows, rows)
                    pairs.append((piece_ref.at[zs, i * rows : (i + 1) * rows], t_ref.at[zs, pl.ds(to, rows)]))
            return [pltpu.make_async_copy(*pair, sems.at[g, n]) for n, pair in enumerate(pairs)]

        @pl.loop(0, groups)
        def _(g):
            for copy in copies(g):
                copy.start()

        acc_ref[...] = jnp.zeros_like(acc_ref)

        @pl.loop(0, groups)
        def _(g):
            for copy in copies(g):
                copy.wait()
            for side in range(2):
                term = None
                for j in range(TOGETHER):
                    product = lax.dot_general(
                        w_ref[side, g * TOGETHER + j], t_ref[g * TOGETHER + j],
                        (((1,), (1,)), ((), ())), preferred_element_type=F32,
                    )
                    term = product if term is None else term + product
                acc_ref[side] += term

        kept = jnp.where(place_ref[2] == place_ref[4], 0, 1)
        keep_ref[...] = acc_ref[kept]
        give_ref[...] = acc_ref[1 - kept]

    out = jax.ShapeDtypeStruct((units, width), F32)
    args = (own, other, *pieces)
    return pl.pallas_call(
        body,
        in_specs=[SCALARS] + [pl.BlockSpec(memory_space=pl.ANY)] * 10,
        out_specs=[WHOLE] * 2,
        out_shape=[out] * 2,
        scratch_shapes=[
            pltpu.VMEM((nz, width, depth), BF16),
            pltpu.VMEM((2, nz, units, depth), BF16),
            pltpu.VMEM((2, units, width), F32),
            pltpu.SemaphoreType.DMA((groups, 18)),
        ],
        cost_estimate=cost(4 * nz * units * depth * width, *args),
        name="project",
        compiler_params=room(22),
    )(place, *args)


def activate(keep, got):
    units, rows = keep.shape[0] // 2, keep.shape[1]

    def body(keep_ref, got_ref, o_ref):
        gate = keep_ref[:units] + got_ref[:units]
        up = keep_ref[units:] + got_ref[units:]
        o_ref[...] = (gate / (1 + jnp.exp(-gate)) * up).astype(o_ref.dtype)

    return pl.pallas_call(
        body,
        in_specs=[WHOLE] * 2,
        out_specs=WHOLE,
        out_shape=jax.ShapeDtypeStruct((units, rows), BF16),
        cost_estimate=cost(0, keep, got),
        name="activate",
        compiler_params=room(6),
    )(keep, got)


def mix(place, chunk, rings, mine, theirs):
    nz = SIZES[3]
    sizes = [ring[0].shape[0] for ring in rings]
    units, rows = sum(sizes), rings[0][0].shape[1] // CHUNKS
    width = mine.shape[1]
    order = (0, 1, 2, 3, 4, -4, -3, -2, -1)
    parts = [ring[s] for ring in rings for s in order]

    def body(place_ref, mine_ref, theirs_ref, *rest):
        part_refs, (o_ref, h_ref) = list(rest[:-2]), rest[-2:]
        c, z = place_ref[2], place_ref[3]
        first = 0
        for size in sizes:
            for s in order:
                length = size // 2 if abs(s) == nz // 2 else size
                at = ((z - s + nz) % nz) * units + first + (length if s == -nz // 2 else 0)
                h_ref[pl.ds(pl.multiple_of(at, 16), length)] = part_refs.pop(0)[...]
            first += size
        for side, w_ref in ((c, mine_ref), (1 - c, theirs_ref)):
            o_ref[side] = lax.dot_general(
                h_ref[...], w_ref[...], (((0,), (0,)), ((), ())), preferred_element_type=F32
            ).astype(o_ref.dtype)

    return pl.pallas_call(
        body,
        grid=(1,),
        in_specs=[SCALARS]
        + [pl.BlockSpec(mine.shape, lambda k: (0, 0))] * 2
        + [pl.BlockSpec((p.shape[0], rows), lambda k: (0, chunk)) for p in parts],
        out_specs=pl.BlockSpec((2, rows, width), lambda k: (0, 0, 0)),
        out_shape=jax.ShapeDtypeStruct((2, rows, width), BF16),
        scratch_shapes=[pltpu.VMEM((nz * units, rows), BF16)],
        cost_estimate=cost(4 * nz * units * rows * width, mine, theirs, *parts),
        name="mix",
        compiler_params=room(16),
    )(place, mine, theirs, *parts)


def shards(tokens, gate_weight, up_weight, down_weight):
    xl, y, c, z, xh = (lax.axis_index(a) for a in AXES)
    place = jnp.stack([xl, y, c, z, xh]).astype(jnp.int32)
    nz = SIZES[3]
    rows = tokens.shape[0] // CHUNKS

    around = {0: tokens}
    for s in (1, -1, 2, -2, 4):
        around[s] = along_z(tokens, s)
    around[3], around[-3] = along_z(around[2], 1), along_z(around[-2], -1)
    sliced = slice_units(gate_weight, up_weight, nz)
    ready, *around = together(sliced[0], *(around[s] for s in (0, 1, 2, 3, 4, -3, -2, -1)))
    weights = [lax.all_to_all(ready, "z", 0, 0, tiled=True)]

    near = regroup(place, around)
    far = swap_xl(near)
    near_before, near_after = along_y(near, 1), along_y(near, -1)
    far_before, far_after = along_y(far, 1), along_y(far, -1)
    near_across, far_across = along_y(near_before, 1), along_y(far_after, -1)
    ready, weights[0], near_across, far_across = together(sliced[1], weights[0], near_across, far_across)
    weights.append(lax.all_to_all(ready, "z", 0, 0, tiled=True))
    pieces = (near, far, near_after, far_after, near_across, far_across, near_before, far_before)

    def sums(weight):
        return project(place, weight, swap_core(weight), pieces)

    keep, give = sums(weights[0])
    got = swap_xh(give)
    hiddens = [activate(keep, got)]

    down_weight, _ = together(down_weight, far)
    moved = send(
        down_weight,
        lambda xl, y, c, z, xh: (xl, y, 1 - c, z, 1 - xh) if c != xh else None,
    )
    moved, weights[1], _ = together(moved, weights[1], got)
    mine = jnp.where(c == xh, down_weight, moved)
    keep, give = sums(weights[1])
    hiddens.append(activate(keep, swap_xh(give)))
    mine, _ = together(mine, give)
    theirs = swap_core(mine)

    rings = []
    for hidden in hiddens:
        ring, up, down = {0: hidden}, hidden, hidden
        for at in range(nz // 2):
            if at == nz // 2 - 1:
                half = up.shape[0] // 2
                up, down = up[:half], down[half:]
            up, down = along_z(up, 1), along_z(down, -1)
            ring.update({at + 1: up, -at - 1: down})
        rings.append(ring)

    outs = []
    for i in range(CHUNKS):
        out = mix(place, i, rings, mine, theirs).reshape(16, rows, -1)
        got = lax.all_to_all(out, ("xh", "y", "xl"), 0, 0, tiled=True)
        outs.append(jnp.sum(got.astype(F32), 0))
    return jnp.concatenate(outs)


def solution(mesh):
    split = Mesh(mesh.devices.reshape(SIZES), AXES)
    row, col = ("xl", "y", "c"), ("z", "xh")
    return jax.shard_map(
        shards,
        mesh=split,
        in_specs=(P(row, col), P(col, row), P(col, row), P(row, col)),
        out_specs=P(row, col),
        check_vma=False,
    )
```

```python
import functools
import itertools

import jax
import jax.numpy as jnp
from jax import lax
from jax.experimental import pallas as pl
from jax.experimental.pallas import tpu as pltpu
from jax.sharding import Mesh, PartitionSpec as P

AXES = ("xl", "y", "c", "z", "xh")
SIZES = (2, 4, 2, 8, 2)
FIRST = 160
TOGETHER = 2
F32, BF16 = jnp.float32, jnp.bfloat16
SCALARS = pl.BlockSpec(memory_space=pltpu.SMEM)
WHOLE = pl.BlockSpec(memory_space=pltpu.VMEM)


def send(value, move):
    flat = lambda at: sum(i * k for i, k in zip(at, (128, 32, 16, 2, 1)))
    pairs = []
    for at in itertools.product(*map(range, SIZES)):
        to = move(*at)
        if to is not None:
            pairs.append((flat(at), flat(tuple(i % n for i, n in zip(to, SIZES)))))
    return lax.ppermute(value, AXES, pairs)


def along_z(value, step):
    return send(value, lambda xl, y, c, z, xh: (xl, y, c, z + step, xh))


def along_y(value, step):
    return send(value, lambda xl, y, c, z, xh: (xl, y + step, c, z, xh))


def swap_xl(value):
    return send(value, lambda xl, y, c, z, xh: (1 - xl, y, c, z, xh))


def swap_xh(value):
    return send(value, lambda xl, y, c, z, xh: (xl, y, c, z, 1 - xh))


def swap_core(value):
    return send(value, lambda xl, y, c, z, xh: (xl, y, 1 - c, z, xh))


def together(*values):
    return lax.optimization_barrier(values)


def cost(flops, *arrays):
    size = sum(a.size * a.dtype.itemsize for a in arrays)
    return pl.CostEstimate(flops=flops // 64, bytes_accessed=size // 64, transcendentals=0)


def regroup(place, parts):
    nz = SIZES[3]

    def body(place_ref, *rest):
        z = place_ref[3]
        for s, part_ref in enumerate(rest[:nz]):
            rest[nz][(z + nz - s) % nz] = part_ref[...]

    return pl.pallas_call(
        body,
        in_specs=[SCALARS] + [WHOLE] * nz,
        out_specs=WHOLE,
        out_shape=jax.ShapeDtypeStruct((nz, *parts[0].shape), BF16),
        cost_estimate=cost(0, *parts, *parts),
        name="regroup",
    )(place, *parts)


def slice_units(gate, up, nz):
    depth, width = gate.shape
    units = width // nz
    step = 256
    cuts = ((0, FIRST), (FIRST, units))

    def body(g_ref, u_ref, *o_refs):
        for w_ref, at in ((g_ref, 0), (u_ref, 1)):
            w = w_ref[...].T.reshape(nz, units, step)
            for (lo, hi), o_ref in zip(cuts, o_refs):
                o_ref[:, at * (hi - lo) : (at + 1) * (hi - lo)] = w[:, lo:hi]

    outs = [jax.ShapeDtypeStruct((nz, 2 * (hi - lo), depth), gate.dtype) for lo, hi in cuts]
    return pl.pallas_call(
        body,
        grid=(depth // step,),
        in_specs=[pl.BlockSpec((step, width), lambda k: (k, 0))] * 2,
        out_specs=[pl.BlockSpec((*o.shape[:2], step), lambda k: (0, 0, k)) for o in outs],
        out_shape=outs,
        cost_estimate=cost(0, gate, up, *outs),
        name="slice_units",
    )(gate, up)


def project(place, own, other, pieces, cuts):
    nz, units, depth = own.shape
    rows = pieces[0].shape[1]
    width = 8 * rows
    groups = nz // TOGETHER

    def body(place_ref, own_ref, other_ref, *rest):
        piece_refs, (keep_ref, *give_refs, t_ref, w_ref, acc_ref, sems) = rest[:8], rest[8:]
        xl, y = place_ref[0], place_ref[1]

        def copies(g):
            zs = pl.ds(g * TOGETHER, TOGETHER)
            pairs = [
                (own_ref.at[zs], w_ref.at[zs, pl.ds(0, units)]),
                (other_ref.at[zs], w_ref.at[zs, pl.ds(units, units)]),
            ]
            for n, piece_ref in enumerate(piece_refs):
                at = ((y + n // 2) % 4) * 2 + (xl + n % 2) % 2
                to = pl.multiple_of(at * rows, rows)
                pairs.append((piece_ref.at[zs], t_ref.at[zs, pl.ds(to, rows)]))
            return [pltpu.make_async_copy(*pair, sems.at[g, n]) for n, pair in enumerate(pairs)]

        @pl.loop(0, groups)
        def _(g):
            for copy in copies(g):
                copy.start()

        acc_ref[...] = jnp.zeros_like(acc_ref)

        @pl.loop(0, groups)
        def _(g):
            for copy in copies(g):
                copy.wait()
            for j in range(TOGETHER):
                acc_ref[...] += lax.dot_general(
                    w_ref[g * TOGETHER + j], t_ref[g * TOGETHER + j],
                    (((1,), (1,)), ((), ())), preferred_element_type=F32,
                )

        kept = pl.multiple_of(jnp.where(place_ref[2] == place_ref[4], 0, units), units)
        keep_ref[...] = acc_ref[pl.ds(kept, units)]
        for lo, hi, give_ref in zip((0, *cuts), (*cuts, units), give_refs):
            give_ref[...] = acc_ref[pl.ds(pl.multiple_of(units - kept + lo, 8), hi - lo)]

    outs = [
        jax.ShapeDtypeStruct((hi - lo, width), F32)
        for lo, hi in ((0, units), *zip((0, *cuts), (*cuts, units)))
    ]
    args = (own, other, *pieces)
    return pl.pallas_call(
        body,
        in_specs=[SCALARS] + [pl.BlockSpec(memory_space=pl.ANY)] * 10,
        out_specs=[WHOLE] * len(outs),
        out_shape=outs,
        scratch_shapes=[
            pltpu.VMEM((nz, width, depth), BF16),
            pltpu.VMEM((nz, 2 * units, depth), BF16),
            pltpu.VMEM((2 * units, width), F32),
            pltpu.SemaphoreType.DMA((groups, 10)),
        ],
        cost_estimate=cost(4 * nz * units * depth * width, *args),
        name="project",
    )(place, *args)


def activate(keep, gots):
    units, rows = keep.shape[0] // 2, keep.shape[1]

    def body(keep_ref, *rest):
        got_refs, (o_ref, sum_ref) = rest[:-2], rest[-2:]
        at = 0
        for got_ref in got_refs:
            here = slice(at, at + got_ref.shape[0])
            sum_ref[here] = keep_ref[here] + got_ref[...]
            at += got_ref.shape[0]
        gate, up = sum_ref[:units], sum_ref[units:]
        o_ref[...] = (gate / (1 + jnp.exp(-gate)) * up).astype(o_ref.dtype)

    return pl.pallas_call(
        body,
        in_specs=[WHOLE] * (1 + len(gots)),
        out_specs=WHOLE,
        out_shape=jax.ShapeDtypeStruct((units, rows), BF16),
        scratch_shapes=[pltpu.VMEM(keep.shape, F32)],
        cost_estimate=cost(0, keep, *gots),
        name="activate",
    )(keep, *gots)


def mix(place, rings, mine, theirs):
    nz = SIZES[3]
    sizes = [ring[0].shape[0] for ring in rings]
    units, rows = sum(sizes), rings[0][0].shape[1]
    width = mine.shape[1]
    order = (0, 1, 2, 3, 4, -4, -3, -2, -1)
    parts = [ring[s] for ring in rings for s in order]

    def body(place_ref, mine_ref, theirs_ref, *rest):
        part_refs, (o_ref, h_ref) = list(rest[:-2]), rest[-2:]
        c, z = place_ref[2], place_ref[3]
        first = 0
        for size in sizes:
            for s in order:
                length = size // 2 if abs(s) == nz // 2 else size
                at = ((z - s + nz) % nz) * units + first + (length if s == -nz // 2 else 0)
                h_ref[pl.ds(pl.multiple_of(at, 16), length)] = part_refs.pop(0)[...]
            first += size
        for side, w_ref in ((c, mine_ref), (1 - c, theirs_ref)):
            o_ref[side] = lax.dot_general(
                h_ref[...], w_ref[...], (((0,), (0,)), ((), ())), preferred_element_type=F32
            ).astype(o_ref.dtype)

    return pl.pallas_call(
        body,
        in_specs=[SCALARS] + [WHOLE] * (2 + len(parts)),
        out_specs=WHOLE,
        out_shape=jax.ShapeDtypeStruct((2, rows, width), BF16),
        scratch_shapes=[pltpu.VMEM((nz * units, rows), BF16)],
        cost_estimate=cost(4 * nz * units * rows * width, mine, theirs, *parts),
        name="mix",
    )(place, mine, theirs, *parts)


def shards(tokens, gate_weight, up_weight, down_weight):
    xl, y, c, z, xh = (lax.axis_index(a) for a in AXES)
    place = jnp.stack([xl, y, c, z, xh]).astype(jnp.int32)
    nz = SIZES[3]

    around = {0: tokens}
    for s in (1, -1, 2, -2, 4):
        around[s] = along_z(tokens, s)
    around[3], around[-3] = along_z(around[2], 1), along_z(around[-2], -1)
    sliced = slice_units(gate_weight, up_weight, nz)
    ready, *around = together(sliced[0], *(around[s] for s in (0, 1, 2, 3, 4, -3, -2, -1)))
    weights = [lax.all_to_all(ready, "z", 0, 0, tiled=True)]

    near = regroup(place, around)
    far = swap_xl(near)
    near_before, near_after = along_y(near, 1), along_y(near, -1)
    far_before, far_after = along_y(far, 1), along_y(far, -1)
    near_across, far_across = along_y(near_before, 1), along_y(far_after, -1)
    pieces = (near, far, near_after, far_after, near_across, far_across, near_before, far_before)
    ready, weights[0], pieces = together(sliced[1], weights[0], pieces)
    weights.append(lax.all_to_all(ready, "z", 0, 0, tiled=True))

    keep, *gives = project(place, weights[0], swap_core(weights[0]), pieces, ())
    gots = [swap_xh(give) for give in gives]
    hiddens = [activate(keep, gots)]

    down_weight, _ = together(down_weight, far)
    moved = send(
        down_weight,
        lambda xl, y, c, z, xh: (xl, y, 1 - c, z, 1 - xh) if c != xh else None,
    )
    moved, weights[1], _ = together(moved, weights[1], gives[0])
    mine = jnp.where(c == xh, down_weight, moved)

    keep, give = project(place, weights[1], swap_core(weights[1]), pieces, ())
    hiddens.append(activate(keep, [swap_xh(give)]))
    mine, _ = together(mine, give)
    theirs = swap_core(mine)

    rings = []
    for hidden in hiddens:
        ring, up, down = {0: hidden}, hidden, hidden
        for at in range(nz // 2):
            if at == nz // 2 - 1:
                half = up.shape[0] // 2
                up, down = up[:half], down[half:]
            up, down = along_z(up, 1), along_z(down, -1)
            ring.update({at + 1: up, -at - 1: down})
        rings.append(ring)

    out = mix(place, rings, mine, theirs).reshape(16, tokens.shape[0], -1)
    got = lax.all_to_all(out, ("xh", "y", "xl"), 0, 0, tiled=True)
    return jnp.sum(got.astype(F32), 0)


def solution(mesh):
    split = Mesh(mesh.devices.reshape(SIZES), AXES)
    row, col = ("xl", "y", "c"), ("z", "xh")
    return jax.shard_map(
        shards,
        mesh=split,
        in_specs=(P(row, col), P(col, row), P(col, row), P(row, col)),
        out_specs=P(row, col),
        check_vma=False,
    )
```

```python
import functools
import itertools

import jax
import jax.numpy as jnp
from jax import lax
from jax.experimental import pallas as pl
from jax.experimental.pallas import tpu as pltpu
from jax.sharding import Mesh, PartitionSpec as P

AXES = ("xl", "y", "c", "z", "xh")
SIZES = (2, 4, 2, 8, 2)
FIRST = 160
TOGETHER = 2
F32, BF16 = jnp.float32, jnp.bfloat16
SCALARS = pl.BlockSpec(memory_space=pltpu.SMEM)
WHOLE = pl.BlockSpec(memory_space=pltpu.VMEM)


def send(value, move):
    flat = lambda at: sum(i * k for i, k in zip(at, (128, 32, 16, 2, 1)))
    pairs = []
    for at in itertools.product(*map(range, SIZES)):
        to = move(*at)
        if to is not None:
            pairs.append((flat(at), flat(tuple(i % n for i, n in zip(to, SIZES)))))
    return lax.ppermute(value, AXES, pairs)


def along_z(value, step):
    return send(value, lambda xl, y, c, z, xh: (xl, y, c, z + step, xh))


def along_y(value, step):
    return send(value, lambda xl, y, c, z, xh: (xl, y + step, c, z, xh))


def swap_xl(value):
    return send(value, lambda xl, y, c, z, xh: (1 - xl, y, c, z, xh))


def swap_xh(value):
    return send(value, lambda xl, y, c, z, xh: (xl, y, c, z, 1 - xh))


def swap_core(value):
    return send(value, lambda xl, y, c, z, xh: (xl, y, 1 - c, z, xh))


def together(*values):
    return lax.optimization_barrier(values)


def room(mib):
    return pltpu.CompilerParams(vmem_limit_bytes=mib << 20)


def cost(flops, *arrays):
    size = sum(a.size * a.dtype.itemsize for a in arrays)
    return pl.CostEstimate(flops=flops // 64, bytes_accessed=size // 64, transcendentals=0)


def regroup(place, parts):
    nz = SIZES[3]

    def body(place_ref, *rest):
        z = place_ref[3]
        for s, part_ref in enumerate(rest[:nz]):
            rest[nz][(z + nz - s) % nz] = part_ref[...]

    return pl.pallas_call(
        body,
        in_specs=[SCALARS] + [WHOLE] * nz,
        out_specs=WHOLE,
        out_shape=jax.ShapeDtypeStruct((nz, *parts[0].shape), BF16),
        cost_estimate=cost(0, *parts, *parts),
        name="regroup",
    )(place, *parts)


def slice_units(gate, up, nz):
    depth, width = gate.shape
    units = width // nz
    step = 256
    cuts = ((0, FIRST), (FIRST, units))

    def body(g_ref, u_ref, *o_refs):
        for w_ref, at in ((g_ref, 0), (u_ref, 1)):
            w = w_ref[...].T.reshape(nz, units, step)
            for (lo, hi), o_ref in zip(cuts, o_refs):
                o_ref[:, at * (hi - lo) : (at + 1) * (hi - lo)] = w[:, lo:hi]

    outs = [jax.ShapeDtypeStruct((nz, 2 * (hi - lo), depth), gate.dtype) for lo, hi in cuts]
    return pl.pallas_call(
        body,
        grid=(depth // step,),
        in_specs=[pl.BlockSpec((step, width), lambda k: (k, 0))] * 2,
        out_specs=[pl.BlockSpec((*o.shape[:2], step), lambda k: (0, 0, k)) for o in outs],
        out_shape=outs,
        cost_estimate=cost(0, gate, up, *outs),
        name="slice_units",
    )(gate, up)


def project(place, own, other, pieces, cuts):
    nz, units, depth = own.shape
    rows = pieces[0].shape[1]
    width = 8 * rows
    groups = nz // TOGETHER

    def body(place_ref, own_ref, other_ref, *rest):
        piece_refs, (keep_ref, *give_refs, t_ref, w_ref, acc_ref, sems) = rest[:8], rest[8:]
        xl, y = place_ref[0], place_ref[1]

        def copies(g):
            zs = pl.ds(g * TOGETHER, TOGETHER)
            pairs = [
                (own_ref.at[zs], w_ref.at[zs, pl.ds(0, units)]),
                (other_ref.at[zs], w_ref.at[zs, pl.ds(units, units)]),
            ]
            for n, piece_ref in enumerate(piece_refs):
                at = ((y + n // 2) % 4) * 2 + (xl + n % 2) % 2
                to = pl.multiple_of(at * rows, rows)
                pairs.append((piece_ref.at[zs], t_ref.at[zs, pl.ds(to, rows)]))
            return [pltpu.make_async_copy(*pair, sems.at[g, n]) for n, pair in enumerate(pairs)]

        @pl.loop(0, groups)
        def _(g):
            for copy in copies(g):
                copy.start()

        acc_ref[...] = jnp.zeros_like(acc_ref)

        @pl.loop(0, groups)
        def _(g):
            for copy in copies(g):
                copy.wait()
            for j in range(TOGETHER):
                acc_ref[...] += lax.dot_general(
                    w_ref[g * TOGETHER + j], t_ref[g * TOGETHER + j],
                    (((1,), (1,)), ((), ())), preferred_element_type=F32,
                )

        kept = pl.multiple_of(jnp.where(place_ref[2] == place_ref[4], 0, units), units)
        keep_ref[...] = acc_ref[pl.ds(kept, units)]
        for lo, hi, give_ref in zip((0, *cuts), (*cuts, units), give_refs):
            give_ref[...] = acc_ref[pl.ds(pl.multiple_of(units - kept + lo, 8), hi - lo)]

    outs = [
        jax.ShapeDtypeStruct((hi - lo, width), F32)
        for lo, hi in ((0, units), *zip((0, *cuts), (*cuts, units)))
    ]
    args = (own, other, *pieces)
    return pl.pallas_call(
        body,
        in_specs=[SCALARS] + [pl.BlockSpec(memory_space=pl.ANY)] * 10,
        out_specs=[WHOLE] * len(outs),
        out_shape=outs,
        scratch_shapes=[
            pltpu.VMEM((nz, width, depth), BF16),
            pltpu.VMEM((nz, 2 * units, depth), BF16),
            pltpu.VMEM((2 * units, width), F32),
            pltpu.SemaphoreType.DMA((groups, 10)),
        ],
        cost_estimate=cost(4 * nz * units * depth * width, *args),
        name="project",
    )(place, *args)


def activate(keep, gots):
    units, rows = keep.shape[0] // 2, keep.shape[1]

    def body(keep_ref, *rest):
        got_refs, (o_ref, sum_ref) = rest[:-2], rest[-2:]
        at = 0
        for got_ref in got_refs:
            here = slice(at, at + got_ref.shape[0])
            sum_ref[here] = keep_ref[here] + got_ref[...]
            at += got_ref.shape[0]
        gate, up = sum_ref[:units], sum_ref[units:]
        o_ref[...] = (gate / (1 + jnp.exp(-gate)) * up).astype(o_ref.dtype)

    return pl.pallas_call(
        body,
        in_specs=[WHOLE] * (1 + len(gots)),
        out_specs=WHOLE,
        out_shape=jax.ShapeDtypeStruct((units, rows), BF16),
        scratch_shapes=[pltpu.VMEM(keep.shape, F32)],
        cost_estimate=cost(0, keep, *gots),
        name="activate",
        compiler_params=room(8),
    )(keep, *gots)


def mix(place, rings, mine, theirs):
    nz = SIZES[3]
    sizes = [ring[0].shape[0] for ring in rings]
    units, rows = sum(sizes), rings[0][0].shape[1]
    width = mine.shape[1]
    order = (0, 1, 2, 3, 4, -4, -3, -2, -1)
    parts = [ring[s] for ring in rings for s in order]

    def body(place_ref, mine_ref, theirs_ref, *rest):
        part_refs, (o_ref, h_ref) = list(rest[:-2]), rest[-2:]
        c, z = place_ref[2], place_ref[3]
        first = 0
        for size in sizes:
            for s in order:
                length = size // 2 if abs(s) == nz // 2 else size
                at = ((z - s + nz) % nz) * units + first + (length if s == -nz // 2 else 0)
                h_ref[pl.ds(pl.multiple_of(at, 16), length)] = part_refs.pop(0)[...]
            first += size
        for side, w_ref in ((c, mine_ref), (1 - c, theirs_ref)):
            o_ref[side] = lax.dot_general(
                h_ref[...], w_ref[...], (((0,), (0,)), ((), ())), preferred_element_type=F32
            ).astype(o_ref.dtype)

    return pl.pallas_call(
        body,
        in_specs=[SCALARS] + [WHOLE] * (2 + len(parts)),
        out_specs=WHOLE,
        out_shape=jax.ShapeDtypeStruct((2, rows, width), BF16),
        scratch_shapes=[pltpu.VMEM((nz * units, rows), BF16)],
        cost_estimate=cost(4 * nz * units * rows * width, mine, theirs, *parts),
        name="mix",
        compiler_params=room(24),
    )(place, mine, theirs, *parts)


def shards(tokens, gate_weight, up_weight, down_weight):
    xl, y, c, z, xh = (lax.axis_index(a) for a in AXES)
    place = jnp.stack([xl, y, c, z, xh]).astype(jnp.int32)
    nz = SIZES[3]

    around = {0: tokens}
    for s in (1, -1, 2, -2, 4):
        around[s] = along_z(tokens, s)
    around[3], around[-3] = along_z(around[2], 1), along_z(around[-2], -1)
    sliced = slice_units(gate_weight, up_weight, nz)
    ready, *around = together(sliced[0], *(around[s] for s in (0, 1, 2, 3, 4, -3, -2, -1)))
    weights = [lax.all_to_all(ready, "z", 0, 0, tiled=True)]

    near = regroup(place, around)
    far = swap_xl(near)
    near_before, near_after = along_y(near, 1), along_y(near, -1)
    far, near_before, near_after = together(far, near_before, near_after)
    far_before, far_after = along_y(far, 1), along_y(far, -1)
    near_across, far_across = along_y(near_before, 1), along_y(far_after, -1)
    pieces = (near, far, near_after, far_after, near_across, far_across, near_before, far_before)
    ready, weights[0], pieces = together(sliced[1], weights[0], pieces)
    weights.append(lax.all_to_all(ready, "z", 0, 0, tiled=True))

    keep, *gives = project(place, weights[0], swap_core(weights[0]), pieces, ())
    gots = [swap_xh(give) for give in gives]
    hiddens = [activate(keep, gots)]

    down_weight, _ = together(down_weight, far)
    moved = send(
        down_weight,
        lambda xl, y, c, z, xh: (xl, y, 1 - c, z, 1 - xh) if c != xh else None,
    )
    moved, weights[1], _ = together(moved, weights[1], gots[0])
    mine = jnp.where(c == xh, down_weight, moved)

    both = together(weights[1], swap_core(weights[1]), hiddens[0])
    keep, give = project(place, *both[:2], pieces, ())
    hiddens.append(activate(keep, [swap_xh(give)]))
    mine, _ = together(mine, give)
    theirs = swap_core(mine)

    rings = []
    for hidden in hiddens:
        ring, up, down = {0: hidden}, hidden, hidden
        for at in range(nz // 2):
            if at == nz // 2 - 1:
                half = up.shape[0] // 2
                up, down = up[:half], down[half:]
            up, down = along_z(up, 1), along_z(down, -1)
            ring.update({at + 1: up, -at - 1: down})
        rings.append(ring)

    out = mix(place, rings, mine, theirs).reshape(16, tokens.shape[0], -1)
    got = lax.all_to_all(out, ("xh", "y", "xl"), 0, 0, tiled=True)
    return jnp.sum(got.astype(F32), 0)


def solution(mesh):
    split = Mesh(mesh.devices.reshape(SIZES), AXES)
    row, col = ("xl", "y", "c"), ("z", "xh")
    return jax.shard_map(
        shards,
        mesh=split,
        in_specs=(P(row, col), P(col, row), P(col, row), P(row, col)),
        out_specs=P(row, col),
        check_vma=False,
    )
```

```python
import functools
import itertools

import jax
import jax.numpy as jnp
from jax import lax
from jax.experimental import pallas as pl
from jax.experimental.pallas import tpu as pltpu
from jax.sharding import Mesh, PartitionSpec as P

AXES = ("xl", "y", "c", "z", "xh")
SIZES = (2, 4, 2, 8, 2)
FIRST = 128
TOGETHER = 2
F32, BF16 = jnp.float32, jnp.bfloat16
SCALARS = pl.BlockSpec(memory_space=pltpu.SMEM)
WHOLE = pl.BlockSpec(memory_space=pltpu.VMEM)


def send(value, move):
    flat = lambda at: sum(i * k for i, k in zip(at, (128, 32, 16, 2, 1)))
    pairs = []
    for at in itertools.product(*map(range, SIZES)):
        to = move(*at)
        if to is not None:
            pairs.append((flat(at), flat(tuple(i % n for i, n in zip(to, SIZES)))))
    return lax.ppermute(value, AXES, pairs)


def along_z(value, step):
    return send(value, lambda xl, y, c, z, xh: (xl, y, c, z + step, xh))


def along_y(value, step):
    return send(value, lambda xl, y, c, z, xh: (xl, y + step, c, z, xh))


def swap_xl(value):
    return send(value, lambda xl, y, c, z, xh: (1 - xl, y, c, z, xh))


def swap_xh(value):
    return send(value, lambda xl, y, c, z, xh: (xl, y, c, z, 1 - xh))


def swap_core(value):
    return send(value, lambda xl, y, c, z, xh: (xl, y, 1 - c, z, xh))


def together(*values):
    return lax.optimization_barrier(values)


def room(mib):
    return pltpu.CompilerParams(vmem_limit_bytes=mib << 20)


def cost(flops, *arrays):
    size = sum(a.size * a.dtype.itemsize for a in arrays)
    return pl.CostEstimate(flops=flops // 64, bytes_accessed=size // 64, transcendentals=0)


def regroup(place, parts):
    nz = SIZES[3]

    def body(place_ref, *rest):
        z = place_ref[3]
        for s, part_ref in enumerate(rest[:nz]):
            rest[nz][(z + nz - s) % nz] = part_ref[...]

    return pl.pallas_call(
        body,
        in_specs=[SCALARS] + [WHOLE] * nz,
        out_specs=WHOLE,
        out_shape=jax.ShapeDtypeStruct((nz, *parts[0].shape), BF16),
        cost_estimate=cost(0, *parts, *parts),
        name="regroup",
    )(place, *parts)


def slice_units(gate, up, nz):
    depth, width = gate.shape
    units = width // nz
    step = 256
    cuts = ((0, FIRST), (FIRST, units))

    def body(g_ref, u_ref, *o_refs):
        for w_ref, at in ((g_ref, 0), (u_ref, 1)):
            w = w_ref[...].T.reshape(nz, units, step)
            for (lo, hi), o_ref in zip(cuts, o_refs):
                o_ref[:, at * (hi - lo) : (at + 1) * (hi - lo)] = w[:, lo:hi]

    outs = [jax.ShapeDtypeStruct((nz, 2 * (hi - lo), depth), gate.dtype) for lo, hi in cuts]
    return pl.pallas_call(
        body,
        grid=(depth // step,),
        in_specs=[pl.BlockSpec((step, width), lambda k: (k, 0))] * 2,
        out_specs=[pl.BlockSpec((*o.shape[:2], step), lambda k: (0, 0, k)) for o in outs],
        out_shape=outs,
        cost_estimate=cost(0, gate, up, *outs),
        name="slice_units",
    )(gate, up)


def project(place, own, other, pieces, cuts):
    nz, units, depth = own.shape
    rows = pieces[0].shape[1]
    width = 8 * rows
    groups = nz // TOGETHER

    def body(place_ref, own_ref, other_ref, *rest):
        piece_refs, (keep_ref, *give_refs, t_ref, w_ref, acc_ref, sems) = rest[:8], rest[8:]
        xl, y = place_ref[0], place_ref[1]

        def copies(g):
            zs = pl.ds(g * TOGETHER, TOGETHER)
            pairs = [
                (own_ref.at[zs], w_ref.at[zs, pl.ds(0, units)]),
                (other_ref.at[zs], w_ref.at[zs, pl.ds(units, units)]),
            ]
            for n, piece_ref in enumerate(piece_refs):
                at = ((y + n // 2) % 4) * 2 + (xl + n % 2) % 2
                to = pl.multiple_of(at * rows, rows)
                pairs.append((piece_ref.at[zs], t_ref.at[zs, pl.ds(to, rows)]))
            return [pltpu.make_async_copy(*pair, sems.at[g, n]) for n, pair in enumerate(pairs)]

        @pl.loop(0, groups)
        def _(g):
            for copy in copies(g):
                copy.start()

        acc_ref[...] = jnp.zeros_like(acc_ref)

        @pl.loop(0, groups)
        def _(g):
            for copy in copies(g):
                copy.wait()
            for j in range(TOGETHER):
                acc_ref[...] += lax.dot_general(
                    w_ref[g * TOGETHER + j], t_ref[g * TOGETHER + j],
                    (((1,), (1,)), ((), ())), preferred_element_type=F32,
                )

        kept = pl.multiple_of(jnp.where(place_ref[2] == place_ref[4], 0, units), units)
        keep_ref[...] = acc_ref[pl.ds(kept, units)]
        for lo, hi, give_ref in zip((0, *cuts), (*cuts, units), give_refs):
            give_ref[...] = acc_ref[pl.ds(pl.multiple_of(units - kept + lo, 8), hi - lo)]

    outs = [
        jax.ShapeDtypeStruct((hi - lo, width), F32)
        for lo, hi in ((0, units), *zip((0, *cuts), (*cuts, units)))
    ]
    args = (own, other, *pieces)
    return pl.pallas_call(
        body,
        in_specs=[SCALARS] + [pl.BlockSpec(memory_space=pl.ANY)] * 10,
        out_specs=[WHOLE] * len(outs),
        out_shape=outs,
        scratch_shapes=[
            pltpu.VMEM((nz, width, depth), BF16),
            pltpu.VMEM((nz, 2 * units, depth), BF16),
            pltpu.VMEM((2 * units, width), F32),
            pltpu.SemaphoreType.DMA((groups, 10)),
        ],
        cost_estimate=cost(4 * nz * units * depth * width, *args),
        name="project",
    )(place, *args)


def activate(keep, gots):
    units, rows = keep.shape[0] // 2, keep.shape[1]

    def body(keep_ref, *rest):
        got_refs, (o_ref, sum_ref) = rest[:-2], rest[-2:]
        at = 0
        for got_ref in got_refs:
            here = slice(at, at + got_ref.shape[0])
            sum_ref[here] = keep_ref[here] + got_ref[...]
            at += got_ref.shape[0]
        gate, up = sum_ref[:units], sum_ref[units:]
        o_ref[...] = (gate / (1 + jnp.exp(-gate)) * up).astype(o_ref.dtype)

    return pl.pallas_call(
        body,
        in_specs=[WHOLE] * (1 + len(gots)),
        out_specs=WHOLE,
        out_shape=jax.ShapeDtypeStruct((units, rows), BF16),
        scratch_shapes=[pltpu.VMEM(keep.shape, F32)],
        cost_estimate=cost(0, keep, *gots),
        name="activate",
        compiler_params=room(8),
    )(keep, *gots)


def mix(place, rings, mine, theirs):
    nz = SIZES[3]
    sizes = [ring[0].shape[0] for ring in rings]
    units, rows = sum(sizes), rings[0][0].shape[1]
    width = mine.shape[1]
    order = (0, 1, 2, 3, 4, -4, -3, -2, -1)
    parts = [ring[s] for ring in rings for s in order]

    def body(place_ref, mine_ref, theirs_ref, *rest):
        part_refs, (o_ref, h_ref) = list(rest[:-2]), rest[-2:]
        c, z = place_ref[2], place_ref[3]
        first = 0
        for size in sizes:
            for s in order:
                length = size // 2 if abs(s) == nz // 2 else size
                at = ((z - s + nz) % nz) * units + first + (length if s == -nz // 2 else 0)
                h_ref[pl.ds(pl.multiple_of(at, 16), length)] = part_refs.pop(0)[...]
            first += size
        for side, w_ref in ((c, mine_ref), (1 - c, theirs_ref)):
            o_ref[side] = lax.dot_general(
                h_ref[...], w_ref[...], (((0,), (0,)), ((), ())), preferred_element_type=F32
            ).astype(o_ref.dtype)

    return pl.pallas_call(
        body,
        in_specs=[SCALARS] + [WHOLE] * (2 + len(parts)),
        out_specs=WHOLE,
        out_shape=jax.ShapeDtypeStruct((2, rows, width), BF16),
        scratch_shapes=[pltpu.VMEM((nz * units, rows), BF16)],
        cost_estimate=cost(4 * nz * units * rows * width, mine, theirs, *parts),
        name="mix",
        compiler_params=room(24),
    )(place, mine, theirs, *parts)


def round_z(hidden, other):
    nz = SIZES[3]
    ring, up, down = {0: hidden}, hidden, hidden
    for at in range(nz // 2):
        if at == nz // 2 - 1:
            half = up.shape[0] // 2
            up, down = up[:half], down[half:]
        up, down = along_z(up, 1), along_z(down, -1)
        if at == 1:
            up, down, other = together(up, down, other)
        ring.update({at + 1: up, -at - 1: down})
    return ring, other


def shards(tokens, gate_weight, up_weight, down_weight):
    xl, y, c, z, xh = (lax.axis_index(a) for a in AXES)
    place = jnp.stack([xl, y, c, z, xh]).astype(jnp.int32)
    nz = SIZES[3]

    around = {0: tokens}
    for s in (1, -1, 2, -2, 4):
        around[s] = along_z(tokens, s)
    around[3], around[-3] = along_z(around[2], 1), along_z(around[-2], -1)
    sliced = slice_units(gate_weight, up_weight, nz)
    ready, *around = together(sliced[0], *(around[s] for s in (0, 1, 2, 3, 4, -3, -2, -1)))
    weights = [lax.all_to_all(ready, "z", 0, 0, tiled=True)]

    near = regroup(place, around)
    far = swap_xl(near)
    near_before, near_after = along_y(near, 1), along_y(near, -1)
    far, near_before, near_after = together(far, near_before, near_after)
    far_before, far_after = along_y(far, 1), along_y(far, -1)
    near_across, far_across = along_y(near_before, 1), along_y(far_after, -1)
    pieces = (near, far, near_after, far_after, near_across, far_across, near_before, far_before)
    ready, weights[0], *_ = together(sliced[1], weights[0], far_before, far_after, near_across)
    weights.append(lax.all_to_all(ready, "z", 0, 0, tiled=True))

    keep, *gives = project(place, weights[0], swap_core(weights[0]), pieces, ())
    gots = [swap_xh(give) for give in gives]
    hiddens = [activate(keep, gots)]

    down_weight, _ = together(down_weight, far)
    moved = send(
        down_weight,
        lambda xl, y, c, z, xh: (xl, y, 1 - c, z, 1 - xh) if c != xh else None,
    )
    moved, weights[1], _ = together(moved, weights[1], gots[0])
    mine = jnp.where(c == xh, down_weight, moved)

    both = together(weights[1], swap_core(weights[1]), hiddens[0])
    keep, give = project(place, *both[:2], pieces, ())
    got = swap_xh(give)
    first, (got, mine) = round_z(hiddens[0], (got, mine))
    theirs = swap_core(mine)
    second, _ = round_z(activate(keep, [got]), (first[3], first[-3]))

    out = mix(place, (first, second), mine, theirs).reshape(16, tokens.shape[0], -1)
    got = lax.all_to_all(out, ("xh", "y", "xl"), 0, 0, tiled=True)
    return jnp.sum(got.astype(F32), 0)


def solution(mesh):
    split = Mesh(mesh.devices.reshape(SIZES), AXES)
    row, col = ("xl", "y", "c"), ("z", "xh")
    return jax.shard_map(
        shards,
        mesh=split,
        in_specs=(P(row, col), P(col, row), P(col, row), P(row, col)),
        out_specs=P(row, col),
        check_vma=False,
    )
```

```python
import functools
import itertools

import jax
import jax.numpy as jnp
from jax import lax
from jax.experimental import pallas as pl
from jax.experimental.pallas import tpu as pltpu
from jax.sharding import Mesh, PartitionSpec as P

AXES = ("xl", "y", "c", "z", "xh")
SIZES = (2, 4, 2, 8, 2)
FIRST = 144
TOGETHER = 2
F32, BF16 = jnp.float32, jnp.bfloat16
SCALARS = pl.BlockSpec(memory_space=pltpu.SMEM)
WHOLE = pl.BlockSpec(memory_space=pltpu.VMEM)


def send(value, move):
    flat = lambda at: sum(i * k for i, k in zip(at, (128, 32, 16, 2, 1)))
    pairs = []
    for at in itertools.product(*map(range, SIZES)):
        to = move(*at)
        if to is not None:
            pairs.append((flat(at), flat(tuple(i % n for i, n in zip(to, SIZES)))))
    return lax.ppermute(value, AXES, pairs)


def along_z(value, step):
    return send(value, lambda xl, y, c, z, xh: (xl, y, c, z + step, xh))


def along_y(value, step):
    return send(value, lambda xl, y, c, z, xh: (xl, y + step, c, z, xh))


def swap_xl(value):
    return send(value, lambda xl, y, c, z, xh: (1 - xl, y, c, z, xh))


def swap_xh(value):
    return send(value, lambda xl, y, c, z, xh: (xl, y, c, z, 1 - xh))


def swap_core(value):
    return send(value, lambda xl, y, c, z, xh: (xl, y, 1 - c, z, xh))


def together(*values):
    return lax.optimization_barrier(values)


def room(mib):
    return pltpu.CompilerParams(vmem_limit_bytes=mib << 20)


def cost(flops, *arrays):
    size = sum(a.size * a.dtype.itemsize for a in arrays)
    return pl.CostEstimate(flops=flops // 64, bytes_accessed=size // 64, transcendentals=0)


def regroup(place, parts):
    nz = SIZES[3]

    def body(place_ref, *rest):
        z = place_ref[3]
        for s, part_ref in enumerate(rest[:nz]):
            rest[nz][(z + nz - s) % nz] = part_ref[...]

    return pl.pallas_call(
        body,
        in_specs=[SCALARS] + [WHOLE] * nz,
        out_specs=WHOLE,
        out_shape=jax.ShapeDtypeStruct((nz, *parts[0].shape), BF16),
        cost_estimate=cost(0, *parts, *parts),
        name="regroup",
    )(place, *parts)


def slice_units(gate, up, nz):
    depth, width = gate.shape
    units = width // nz
    step = 256
    cuts = ((0, FIRST), (FIRST, units))

    def body(g_ref, u_ref, *o_refs):
        for w_ref, at in ((g_ref, 0), (u_ref, 1)):
            w = w_ref[...].T.reshape(nz, units, step)
            for (lo, hi), o_ref in zip(cuts, o_refs):
                o_ref[:, at * (hi - lo) : (at + 1) * (hi - lo)] = w[:, lo:hi]

    outs = [jax.ShapeDtypeStruct((nz, 2 * (hi - lo), depth), gate.dtype) for lo, hi in cuts]
    return pl.pallas_call(
        body,
        grid=(depth // step,),
        in_specs=[pl.BlockSpec((step, width), lambda k: (k, 0))] * 2,
        out_specs=[pl.BlockSpec((*o.shape[:2], step), lambda k: (0, 0, k)) for o in outs],
        out_shape=outs,
        cost_estimate=cost(0, gate, up, *outs),
        name="slice_units",
    )(gate, up)


def project(place, own, other, pieces, cuts):
    nz, units, depth = own.shape
    rows = pieces[0].shape[1]
    width = 8 * rows
    groups = nz // TOGETHER

    def body(place_ref, own_ref, other_ref, *rest):
        piece_refs, (keep_ref, *give_refs, t_ref, w_ref, acc_ref, sems) = rest[:8], rest[8:]
        xl, y = place_ref[0], place_ref[1]

        def copies(g):
            zs = pl.ds(g * TOGETHER, TOGETHER)
            pairs = [
                (own_ref.at[zs], w_ref.at[zs, pl.ds(0, units)]),
                (other_ref.at[zs], w_ref.at[zs, pl.ds(units, units)]),
            ]
            for n, piece_ref in enumerate(piece_refs):
                at = ((y + n // 2) % 4) * 2 + (xl + n % 2) % 2
                to = pl.multiple_of(at * rows, rows)
                pairs.append((piece_ref.at[zs], t_ref.at[zs, pl.ds(to, rows)]))
            return [pltpu.make_async_copy(*pair, sems.at[g, n]) for n, pair in enumerate(pairs)]

        @pl.loop(0, groups)
        def _(g):
            for copy in copies(g):
                copy.start()

        acc_ref[...] = jnp.zeros_like(acc_ref)

        @pl.loop(0, groups)
        def _(g):
            for copy in copies(g):
                copy.wait()
            for j in range(TOGETHER):
                acc_ref[...] += lax.dot_general(
                    w_ref[g * TOGETHER + j], t_ref[g * TOGETHER + j],
                    (((1,), (1,)), ((), ())), preferred_element_type=F32,
                )

        kept = pl.multiple_of(jnp.where(place_ref[2] == place_ref[4], 0, units), units)
        keep_ref[...] = acc_ref[pl.ds(kept, units)]
        for lo, hi, give_ref in zip((0, *cuts), (*cuts, units), give_refs):
            give_ref[...] = acc_ref[pl.ds(pl.multiple_of(units - kept + lo, 8), hi - lo)]

    outs = [
        jax.ShapeDtypeStruct((hi - lo, width), F32)
        for lo, hi in ((0, units), *zip((0, *cuts), (*cuts, units)))
    ]
    args = (own, other, *pieces)
    return pl.pallas_call(
        body,
        in_specs=[SCALARS] + [pl.BlockSpec(memory_space=pl.ANY)] * 10,
        out_specs=[WHOLE] * len(outs),
        out_shape=outs,
        scratch_shapes=[
            pltpu.VMEM((nz, width, depth), BF16),
            pltpu.VMEM((nz, 2 * units, depth), BF16),
            pltpu.VMEM((2 * units, width), F32),
            pltpu.SemaphoreType.DMA((groups, 10)),
        ],
        cost_estimate=cost(4 * nz * units * depth * width, *args),
        name="project",
    )(place, *args)


def activate(keep, gots):
    units, rows = keep.shape[0] // 2, keep.shape[1]

    def body(keep_ref, *rest):
        got_refs, (o_ref, sum_ref) = rest[:-2], rest[-2:]
        at = 0
        for got_ref in got_refs:
            here = slice(at, at + got_ref.shape[0])
            sum_ref[here] = keep_ref[here] + got_ref[...]
            at += got_ref.shape[0]
        gate, up = sum_ref[:units], sum_ref[units:]
        o_ref[...] = (gate / (1 + jnp.exp(-gate)) * up).astype(o_ref.dtype)

    return pl.pallas_call(
        body,
        in_specs=[WHOLE] * (1 + len(gots)),
        out_specs=WHOLE,
        out_shape=jax.ShapeDtypeStruct((units, rows), BF16),
        scratch_shapes=[pltpu.VMEM(keep.shape, F32)],
        cost_estimate=cost(0, keep, *gots),
        name="activate",
        compiler_params=room(8),
    )(keep, *gots)


def mix(place, rings, mine, theirs):
    nz = SIZES[3]
    sizes = [ring[0].shape[0] for ring in rings]
    units, rows = sum(sizes), rings[0][0].shape[1]
    width = mine.shape[1]
    order = (0, 1, 2, 3, 4, -4, -3, -2, -1)
    parts = [ring[s] for ring in rings for s in order]

    def body(place_ref, mine_ref, theirs_ref, *rest):
        part_refs, (o_ref, h_ref) = list(rest[:-2]), rest[-2:]
        c, z = place_ref[2], place_ref[3]
        first = 0
        for size in sizes:
            for s in order:
                part_ref = part_refs.pop(0)
                length = part_ref.shape[0]
                at = ((z - s + nz) % nz) * units + first + (size - length if s == -nz // 2 else 0)
                h_ref[pl.ds(pl.multiple_of(at, 16), length)] = part_ref[...]
            first += size
        for side, w_ref in ((c, mine_ref), (1 - c, theirs_ref)):
            o_ref[side] = lax.dot_general(
                h_ref[...], w_ref[...], (((0,), (0,)), ((), ())), preferred_element_type=F32
            ).astype(o_ref.dtype)

    return pl.pallas_call(
        body,
        in_specs=[SCALARS] + [WHOLE] * (2 + len(parts)),
        out_specs=WHOLE,
        out_shape=jax.ShapeDtypeStruct((2, rows, width), BF16),
        scratch_shapes=[pltpu.VMEM((nz * units, rows), BF16)],
        cost_estimate=cost(4 * nz * units * rows * width, mine, theirs, *parts),
        name="mix",
        compiler_params=room(24),
    )(place, mine, theirs, *parts)


def round_z(hidden, other):
    nz = SIZES[3]
    ring, up, down = {0: hidden}, hidden, hidden
    for at in range(nz // 2):
        if at == nz // 2 - 1:
            half = up.shape[0] // 32 * 16
            up, down = up[:half], down[half:]
        up, down = along_z(up, 1), along_z(down, -1)
        if at == 1:
            up, down, other = together(up, down, other)
        ring.update({at + 1: up, -at - 1: down})
    return ring, other


def shards(tokens, gate_weight, up_weight, down_weight):
    xl, y, c, z, xh = (lax.axis_index(a) for a in AXES)
    place = jnp.stack([xl, y, c, z, xh]).astype(jnp.int32)
    nz = SIZES[3]

    around = {0: tokens}
    for s in (1, -1, 2, -2, 4):
        around[s] = along_z(tokens, s)
    around[3], around[-3] = along_z(around[2], 1), along_z(around[-2], -1)
    sliced = slice_units(gate_weight, up_weight, nz)
    near = regroup(place, [around[s] for s in (0, 1, 2, 3, 4, -3, -2, -1)])
    ready, near = together(sliced[0], near)
    weights = [lax.all_to_all(ready, "z", 0, 0, tiled=True)]

    far = swap_xl(near)
    near_before, near_after = along_y(near, 1), along_y(near, -1)
    far, near_before, near_after = together(far, near_before, near_after)
    far_before, far_after = along_y(far, 1), along_y(far, -1)
    near_across, far_across = along_y(near_before, 1), along_y(far_after, -1)
    pieces = (near, far, near_after, far_after, near_across, far_across, near_before, far_before)
    ready, weights[0], pieces = together(sliced[1], weights[0], pieces)
    weights.append(lax.all_to_all(ready, "z", 0, 0, tiled=True))

    keep, *gives = project(place, weights[0], swap_core(weights[0]), pieces, ())
    gots = [swap_xh(give) for give in gives]
    hiddens = [activate(keep, gots)]

    down_weight, _ = together(down_weight, far)
    moved = send(
        down_weight,
        lambda xl, y, c, z, xh: (xl, y, 1 - c, z, 1 - xh) if c != xh else None,
    )
    moved, weights[1], _ = together(moved, weights[1], gots[0])
    mine = jnp.where(c == xh, down_weight, moved)

    both = together(weights[1], swap_core(weights[1]), hiddens[0])
    keep, give = project(place, *both[:2], pieces, ())
    got = swap_xh(give)
    hidden, _ = together(hiddens[0], give)
    first, (got, mine) = round_z(hidden, (got, mine))
    theirs = swap_core(mine)
    second, _ = round_z(activate(keep, [got]), (first[3], first[-3]))

    out = mix(place, (first, second), mine, theirs).reshape(16, tokens.shape[0], -1)
    got = lax.all_to_all(out, ("xh", "y", "xl"), 0, 0, tiled=True)
    return jnp.sum(got.astype(F32), 0)


def solution(mesh):
    split = Mesh(mesh.devices.reshape(SIZES), AXES)
    row, col = ("xl", "y", "c"), ("z", "xh")
    return jax.shard_map(
        shards,
        mesh=split,
        in_specs=(P(row, col), P(col, row), P(col, row), P(row, col)),
        out_specs=P(row, col),
        check_vma=False,
    )
```

```python
import functools
import itertools

import jax
import jax.numpy as jnp
from jax import lax
from jax.experimental import pallas as pl
from jax.experimental.pallas import tpu as pltpu
from jax.sharding import Mesh, PartitionSpec as P

AXES = ("xl", "y", "c", "z", "xh")
SIZES = (2, 4, 2, 8, 2)
FIRST = 144
TOGETHER = 2
F32, BF16 = jnp.float32, jnp.bfloat16
SCALARS = pl.BlockSpec(memory_space=pltpu.SMEM)
WHOLE = pl.BlockSpec(memory_space=pltpu.VMEM)


def send(value, move):
    flat = lambda at: sum(i * k for i, k in zip(at, (128, 32, 16, 2, 1)))
    pairs = []
    for at in itertools.product(*map(range, SIZES)):
        to = move(*at)
        if to is not None:
            pairs.append((flat(at), flat(tuple(i % n for i, n in zip(to, SIZES)))))
    return lax.ppermute(value, AXES, pairs)


def along_z(value, step):
    return send(value, lambda xl, y, c, z, xh: (xl, y, c, z + step, xh))


def along_y(value, step):
    return send(value, lambda xl, y, c, z, xh: (xl, y + step, c, z, xh))


def swap_xl(value):
    return send(value, lambda xl, y, c, z, xh: (1 - xl, y, c, z, xh))


def swap_xh(value):
    return send(value, lambda xl, y, c, z, xh: (xl, y, c, z, 1 - xh))


def swap_core(value):
    return send(value, lambda xl, y, c, z, xh: (xl, y, 1 - c, z, xh))


def together(*values):
    return lax.optimization_barrier(values)


def room(mib):
    return pltpu.CompilerParams(vmem_limit_bytes=mib << 20)


def cost(flops, *arrays):
    size = sum(a.size * a.dtype.itemsize for a in arrays)
    return pl.CostEstimate(flops=flops // 64, bytes_accessed=size // 64, transcendentals=0)


def regroup(place, parts):
    nz = SIZES[3]

    def body(place_ref, *rest):
        z = place_ref[3]
        for s, part_ref in enumerate(rest[:nz]):
            rest[nz][(z + nz - s) % nz] = part_ref[...]

    return pl.pallas_call(
        body,
        in_specs=[SCALARS] + [WHOLE] * nz,
        out_specs=WHOLE,
        out_shape=jax.ShapeDtypeStruct((nz, *parts[0].shape), BF16),
        cost_estimate=cost(0, *parts, *parts),
        name="regroup",
    )(place, *parts)


def slice_units(gate, up, nz):
    depth, width = gate.shape
    units = width // nz
    step = 256
    cuts = ((0, FIRST), (FIRST, units))

    def body(g_ref, u_ref, *o_refs):
        for w_ref, at in ((g_ref, 0), (u_ref, 1)):
            w = w_ref[...].T.reshape(nz, units, step)
            for (lo, hi), o_ref in zip(cuts, o_refs):
                o_ref[:, at * (hi - lo) : (at + 1) * (hi - lo)] = w[:, lo:hi]

    outs = [jax.ShapeDtypeStruct((nz, 2 * (hi - lo), depth), gate.dtype) for lo, hi in cuts]
    return pl.pallas_call(
        body,
        grid=(depth // step,),
        in_specs=[pl.BlockSpec((step, width), lambda k: (k, 0))] * 2,
        out_specs=[pl.BlockSpec((*o.shape[:2], step), lambda k: (0, 0, k)) for o in outs],
        out_shape=outs,
        cost_estimate=cost(0, gate, up, *outs),
        name="slice_units",
    )(gate, up)


def project(place, own, other, pieces, cuts):
    nz, units, depth = own.shape
    rows = pieces[0].shape[1]
    width = 8 * rows
    groups = nz // TOGETHER

    def body(place_ref, own_ref, other_ref, *rest):
        piece_refs, (keep_ref, *give_refs, t_ref, w_ref, acc_ref, sems) = rest[:8], rest[8:]
        xl, y = place_ref[0], place_ref[1]

        def copies(g):
            zs = pl.ds(g * TOGETHER, TOGETHER)
            pairs = [
                (own_ref.at[zs], w_ref.at[zs, pl.ds(0, units)]),
                (other_ref.at[zs], w_ref.at[zs, pl.ds(units, units)]),
            ]
            for n, piece_ref in enumerate(piece_refs):
                at = ((y + n // 2) % 4) * 2 + (xl + n % 2) % 2
                to = pl.multiple_of(at * rows, rows)
                pairs.append((piece_ref.at[zs], t_ref.at[zs, pl.ds(to, rows)]))
            return [pltpu.make_async_copy(*pair, sems.at[g, n]) for n, pair in enumerate(pairs)]

        @pl.loop(0, groups)
        def _(g):
            for copy in copies(g):
                copy.start()

        acc_ref[...] = jnp.zeros_like(acc_ref)

        @pl.loop(0, groups)
        def _(g):
            for copy in copies(g):
                copy.wait()
            for j in range(TOGETHER):
                acc_ref[...] += lax.dot_general(
                    w_ref[g * TOGETHER + j], t_ref[g * TOGETHER + j],
                    (((1,), (1,)), ((), ())), preferred_element_type=F32,
                )

        kept = pl.multiple_of(jnp.where(place_ref[2] == place_ref[4], 0, units), units)
        keep_ref[...] = acc_ref[pl.ds(kept, units)]
        for lo, hi, give_ref in zip((0, *cuts), (*cuts, units), give_refs):
            give_ref[...] = acc_ref[pl.ds(pl.multiple_of(units - kept + lo, 8), hi - lo)]

    outs = [
        jax.ShapeDtypeStruct((hi - lo, width), F32)
        for lo, hi in ((0, units), *zip((0, *cuts), (*cuts, units)))
    ]
    args = (own, other, *pieces)
    return pl.pallas_call(
        body,
        in_specs=[SCALARS] + [pl.BlockSpec(memory_space=pl.ANY)] * 10,
        out_specs=[WHOLE] * len(outs),
        out_shape=outs,
        scratch_shapes=[
            pltpu.VMEM((nz, width, depth), BF16),
            pltpu.VMEM((nz, 2 * units, depth), BF16),
            pltpu.VMEM((2 * units, width), F32),
            pltpu.SemaphoreType.DMA((groups, 10)),
        ],
        cost_estimate=cost(4 * nz * units * depth * width, *args),
        name="project",
    )(place, *args)


def activate(keep, gots):
    units, rows = keep.shape[0] // 2, keep.shape[1]

    def body(keep_ref, *rest):
        got_refs, (o_ref, sum_ref) = rest[:-2], rest[-2:]
        at = 0
        for got_ref in got_refs:
            here = slice(at, at + got_ref.shape[0])
            sum_ref[here] = keep_ref[here] + got_ref[...]
            at += got_ref.shape[0]
        gate, up = sum_ref[:units], sum_ref[units:]
        o_ref[...] = (gate / (1 + jnp.exp(-gate)) * up).astype(o_ref.dtype)

    return pl.pallas_call(
        body,
        in_specs=[WHOLE] * (1 + len(gots)),
        out_specs=WHOLE,
        out_shape=jax.ShapeDtypeStruct((units, rows), BF16),
        scratch_shapes=[pltpu.VMEM(keep.shape, F32)],
        cost_estimate=cost(0, keep, *gots),
        name="activate",
        compiler_params=room(8),
    )(keep, *gots)


def mix(place, rings, mine, theirs):
    nz = SIZES[3]
    sizes = [ring[0].shape[0] for ring in rings]
    units, rows = sum(sizes), rings[0][0].shape[1]
    width = mine.shape[1]
    order = (0, 1, 2, 3, 4, -4, -3, -2, -1)
    parts = [ring[s] for ring in rings for s in order]

    def body(place_ref, mine_ref, theirs_ref, *rest):
        part_refs, (o_ref, h_ref) = list(rest[:-2]), rest[-2:]
        c, z = place_ref[2], place_ref[3]
        first = 0
        for size in sizes:
            for s in order:
                part_ref = part_refs.pop(0)
                length = part_ref.shape[0]
                at = ((z - s + nz) % nz) * units + first + (size - length if s == -nz // 2 else 0)
                h_ref[pl.ds(pl.multiple_of(at, 16), length)] = part_ref[...]
            first += size
        for side, w_ref in ((c, mine_ref), (1 - c, theirs_ref)):
            o_ref[side] = lax.dot_general(
                h_ref[...], w_ref[...], (((0,), (0,)), ((), ())), preferred_element_type=F32
            ).astype(o_ref.dtype)

    return pl.pallas_call(
        body,
        in_specs=[SCALARS] + [WHOLE] * (2 + len(parts)),
        out_specs=WHOLE,
        out_shape=jax.ShapeDtypeStruct((2, rows, width), BF16),
        scratch_shapes=[pltpu.VMEM((nz * units, rows), BF16)],
        cost_estimate=cost(4 * nz * units * rows * width, mine, theirs, *parts),
        name="mix",
        compiler_params=room(24),
    )(place, mine, theirs, *parts)


def round_z(hidden, other):
    nz = SIZES[3]
    ring, up, down = {0: hidden}, hidden, hidden
    for at in range(nz // 2):
        if at == nz // 2 - 1:
            half = up.shape[0] // 32 * 16
            up, down = up[:half], down[half:]
        up, down = along_z(up, 1), along_z(down, -1)
        if at == 1:
            up, down, other = together(up, down, other)
        ring.update({at + 1: up, -at - 1: down})
    return ring, other


def shards(tokens, gate_weight, up_weight, down_weight):
    xl, y, c, z, xh = (lax.axis_index(a) for a in AXES)
    place = jnp.stack([xl, y, c, z, xh]).astype(jnp.int32)
    nz = SIZES[3]

    around = {0: tokens}
    for s in (1, -1, 2, -2, 4):
        around[s] = along_z(tokens, s)
    around[3], around[-3] = along_z(around[2], 1), along_z(around[-2], -1)
    sliced = slice_units(gate_weight, up_weight, nz)
    near = regroup(place, [around[s] for s in (0, 1, 2, 3, 4, -3, -2, -1)])
    ready, near = together(sliced[0], near)
    weights = [lax.all_to_all(ready, "z", 0, 0, tiled=True)]

    far = swap_xl(near)
    near_before, near_after = along_y(near, 1), along_y(near, -1)
    far, near_before, near_after = together(far, near_before, near_after)
    far_before, far_after = along_y(far, 1), along_y(far, -1)
    near_across, far_across = along_y(near_before, 1), along_y(far_after, -1)
    pieces = (near, far, near_after, far_after, near_across, far_across, near_before, far_before)
    down_weight, _ = together(down_weight, far)
    moved = send(
        down_weight,
        lambda xl, y, c, z, xh: (xl, y, 1 - c, z, 1 - xh) if c != xh else None,
    )
    ready, weights[0], pieces, moved = together(sliced[1], weights[0], pieces, moved)
    weights.append(lax.all_to_all(ready, "z", 0, 0, tiled=True))

    keep, *gives = project(place, weights[0], swap_core(weights[0]), pieces, ())
    gots = [swap_xh(give) for give in gives]
    hiddens = [activate(keep, gots)]

    weights[1], _ = together(weights[1], gots[0])
    mine = jnp.where(c == xh, down_weight, moved)

    both = together(weights[1], swap_core(weights[1]), hiddens[0])
    keep, give = project(place, *both[:2], pieces, ())
    got = swap_xh(give)
    hidden, _ = together(hiddens[0], give)
    first, (got, mine) = round_z(hidden, (got, mine))
    theirs = swap_core(mine)
    second, _ = round_z(activate(keep, [got]), (first[3], first[-3]))

    out = mix(place, (first, second), mine, theirs).reshape(16, tokens.shape[0], -1)
    got = lax.all_to_all(out, ("xh", "y", "xl"), 0, 0, tiled=True)
    return jnp.sum(got.astype(F32), 0)


def solution(mesh):
    split = Mesh(mesh.devices.reshape(SIZES), AXES)
    row, col = ("xl", "y", "c"), ("z", "xh")
    return jax.shard_map(
        shards,
        mesh=split,
        in_specs=(P(row, col), P(col, row), P(col, row), P(row, col)),
        out_specs=P(row, col),
        check_vma=False,
    )
```

```python
import functools
import itertools

import jax
import jax.numpy as jnp
from jax import lax
from jax.experimental import pallas as pl
from jax.experimental.pallas import tpu as pltpu
from jax.sharding import Mesh, PartitionSpec as P

AXES = ("xl", "y", "c", "z", "xh")
SIZES = (2, 4, 2, 8, 2)
FIRST = 144
TOGETHER = 2
F32, BF16 = jnp.float32, jnp.bfloat16
SCALARS = pl.BlockSpec(memory_space=pltpu.SMEM)
WHOLE = pl.BlockSpec(memory_space=pltpu.VMEM)


def send(value, move):
    flat = lambda at: sum(i * k for i, k in zip(at, (128, 32, 16, 2, 1)))
    pairs = []
    for at in itertools.product(*map(range, SIZES)):
        to = move(*at)
        if to is not None:
            pairs.append((flat(at), flat(tuple(i % n for i, n in zip(to, SIZES)))))
    return lax.ppermute(value, AXES, pairs)


def along_z(value, step):
    return send(value, lambda xl, y, c, z, xh: (xl, y, c, z + step, xh))


def along_y(value, step):
    return send(value, lambda xl, y, c, z, xh: (xl, y + step, c, z, xh))


def swap_xl(value):
    return send(value, lambda xl, y, c, z, xh: (1 - xl, y, c, z, xh))


def swap_xh(value):
    return send(value, lambda xl, y, c, z, xh: (xl, y, c, z, 1 - xh))


def swap_core(value):
    return send(value, lambda xl, y, c, z, xh: (xl, y, 1 - c, z, xh))


def together(*values):
    return lax.optimization_barrier(values)


def room(mib):
    return pltpu.CompilerParams(vmem_limit_bytes=mib << 20)


def cost(flops, *arrays):
    size = sum(a.size * a.dtype.itemsize for a in arrays)
    return pl.CostEstimate(flops=flops // 64, bytes_accessed=size // 64, transcendentals=0)


def regroup(place, parts):
    nz = SIZES[3]

    def body(place_ref, *rest):
        z = place_ref[3]
        for s, part_ref in enumerate(rest[:nz]):
            rest[nz][(z + nz - s) % nz] = part_ref[...]

    return pl.pallas_call(
        body,
        in_specs=[SCALARS] + [WHOLE] * nz,
        out_specs=WHOLE,
        out_shape=jax.ShapeDtypeStruct((nz, *parts[0].shape), BF16),
        cost_estimate=cost(0, *parts, *parts),
        name="regroup",
    )(place, *parts)


def slice_units(gate, up, nz):
    depth, width = gate.shape
    units = width // nz
    step = 256
    cuts = ((0, FIRST), (FIRST, units))

    def body(g_ref, u_ref, *o_refs):
        for w_ref, at in ((g_ref, 0), (u_ref, 1)):
            w = w_ref[...].T.reshape(nz, units, step)
            for (lo, hi), o_ref in zip(cuts, o_refs):
                o_ref[:, at * (hi - lo) : (at + 1) * (hi - lo)] = w[:, lo:hi]

    outs = [jax.ShapeDtypeStruct((nz, 2 * (hi - lo), depth), gate.dtype) for lo, hi in cuts]
    return pl.pallas_call(
        body,
        grid=(depth // step,),
        in_specs=[pl.BlockSpec((step, width), lambda k: (k, 0))] * 2,
        out_specs=[pl.BlockSpec((*o.shape[:2], step), lambda k: (0, 0, k)) for o in outs],
        out_shape=outs,
        cost_estimate=cost(0, gate, up, *outs),
        name="slice_units",
    )(gate, up)


def project(place, own, other, pieces, cuts):
    nz, units, depth = own.shape
    rows = pieces[0].shape[1]
    width = 8 * rows
    groups = nz // TOGETHER

    def body(place_ref, own_ref, other_ref, *rest):
        piece_refs, (keep_ref, *give_refs, t_ref, w_ref, acc_ref, sems) = rest[:8], rest[8:]
        xl, y = place_ref[0], place_ref[1]

        def copies(g):
            zs = pl.ds(g * TOGETHER, TOGETHER)
            pairs = [
                (own_ref.at[zs], w_ref.at[zs, pl.ds(0, units)]),
                (other_ref.at[zs], w_ref.at[zs, pl.ds(units, units)]),
            ]
            for n, piece_ref in enumerate(piece_refs):
                at = ((y + n // 2) % 4) * 2 + (xl + n % 2) % 2
                to = pl.multiple_of(at * rows, rows)
                pairs.append((piece_ref.at[zs], t_ref.at[zs, pl.ds(to, rows)]))
            return [pltpu.make_async_copy(*pair, sems.at[g, n]) for n, pair in enumerate(pairs)]

        @pl.loop(0, groups)
        def _(g):
            for copy in copies(g):
                copy.start()

        acc_ref[...] = jnp.zeros_like(acc_ref)

        @pl.loop(0, groups)
        def _(g):
            for copy in copies(g):
                copy.wait()
            for j in range(TOGETHER):
                acc_ref[...] += lax.dot_general(
                    w_ref[g * TOGETHER + j], t_ref[g * TOGETHER + j],
                    (((1,), (1,)), ((), ())), preferred_element_type=F32,
                )

        kept = pl.multiple_of(jnp.where(place_ref[2] == place_ref[4], 0, units), units)
        keep_ref[...] = acc_ref[pl.ds(kept, units)]
        for lo, hi, give_ref in zip((0, *cuts), (*cuts, units), give_refs):
            give_ref[...] = acc_ref[pl.ds(pl.multiple_of(units - kept + lo, 8), hi - lo)]

    outs = [
        jax.ShapeDtypeStruct((hi - lo, width), F32)
        for lo, hi in ((0, units), *zip((0, *cuts), (*cuts, units)))
    ]
    args = (own, other, *pieces)
    return pl.pallas_call(
        body,
        in_specs=[SCALARS] + [pl.BlockSpec(memory_space=pl.ANY)] * 10,
        out_specs=[WHOLE] * len(outs),
        out_shape=outs,
        scratch_shapes=[
            pltpu.VMEM((nz, width, depth), BF16),
            pltpu.VMEM((nz, 2 * units, depth), BF16),
            pltpu.VMEM((2 * units, width), F32),
            pltpu.SemaphoreType.DMA((groups, 10)),
        ],
        cost_estimate=cost(4 * nz * units * depth * width, *args),
        name="project",
    )(place, *args)


def activate(keep, gots):
    units, rows = keep.shape[0] // 2, keep.shape[1]

    def body(keep_ref, *rest):
        got_refs, (o_ref, sum_ref) = rest[:-2], rest[-2:]
        at = 0
        for got_ref in got_refs:
            here = slice(at, at + got_ref.shape[0])
            sum_ref[here] = keep_ref[here] + got_ref[...]
            at += got_ref.shape[0]
        gate, up = sum_ref[:units], sum_ref[units:]
        o_ref[...] = (gate / (1 + jnp.exp(-gate)) * up).astype(o_ref.dtype)

    return pl.pallas_call(
        body,
        in_specs=[WHOLE] * (1 + len(gots)),
        out_specs=WHOLE,
        out_shape=jax.ShapeDtypeStruct((units, rows), BF16),
        scratch_shapes=[pltpu.VMEM(keep.shape, F32)],
        cost_estimate=cost(0, keep, *gots),
        name="activate",
        compiler_params=room(8),
    )(keep, *gots)


def mix(place, rings, mine, theirs):
    nz = SIZES[3]
    sizes = [ring[0].shape[0] for ring in rings]
    units, rows = sum(sizes), rings[0][0].shape[1]
    width = mine.shape[1]
    order = (0, 1, 2, 3, 4, -3, -2, -1)
    parts = [ring[s] for ring in rings for s in order]

    def body(place_ref, mine_ref, theirs_ref, *rest):
        part_refs, (o_ref, h_ref) = list(rest[:-2]), rest[-2:]
        c, z = place_ref[2], place_ref[3]
        first = 0
        for size in sizes:
            for s in order:
                at = ((z - s + nz) % nz) * units + first
                h_ref[pl.ds(pl.multiple_of(at, 16), size)] = part_refs.pop(0)[...]
            first += size
        for side, w_ref in ((c, mine_ref), (1 - c, theirs_ref)):
            o_ref[side] = lax.dot_general(
                h_ref[...], w_ref[...], (((0,), (0,)), ((), ())), preferred_element_type=F32
            ).astype(o_ref.dtype)

    return pl.pallas_call(
        body,
        in_specs=[SCALARS] + [WHOLE] * (2 + len(parts)),
        out_specs=WHOLE,
        out_shape=jax.ShapeDtypeStruct((2, rows, width), BF16),
        scratch_shapes=[pltpu.VMEM((nz * units, rows), BF16)],
        cost_estimate=cost(4 * nz * units * rows * width, mine, theirs, *parts),
        name="mix",
        compiler_params=room(24),
    )(place, mine, theirs, *parts)


def round_z(hidden, other, way):
    ring = {0: hidden}
    up = down = hidden
    for at in (1, 2, 3):
        up, down = along_z(up, 1), along_z(down, -1)
        if at == 2:
            up, down, other = together(up, down, other)
        ring.update({at: up, -at: down})
    ring[4] = along_z(up if way > 0 else down, way)
    return ring, other


def shards(tokens, gate_weight, up_weight, down_weight):
    xl, y, c, z, xh = (lax.axis_index(a) for a in AXES)
    place = jnp.stack([xl, y, c, z, xh]).astype(jnp.int32)
    nz = SIZES[3]

    around = {0: tokens}
    for s in (1, -1, 2, -2, 4):
        around[s] = along_z(tokens, s)
    around[3], around[-3] = along_z(around[2], 1), along_z(around[-2], -1)
    sliced = slice_units(gate_weight, up_weight, nz)
    near = regroup(place, [around[s] for s in (0, 1, 2, 3, 4, -3, -2, -1)])
    ready, near = together(sliced[0], near)
    weights = [lax.all_to_all(ready, "z", 0, 0, tiled=True)]

    far = swap_xl(near)
    near_before, near_after = along_y(near, 1), along_y(near, -1)
    far, near_before, near_after = together(far, near_before, near_after)
    far_before, far_after = along_y(far, 1), along_y(far, -1)
    near_across, far_across = along_y(near_before, 1), along_y(far_after, -1)
    pieces = (near, far, near_after, far_after, near_across, far_across, near_before, far_before)
    down_weight, _ = together(down_weight, far)
    moved = send(
        down_weight,
        lambda xl, y, c, z, xh: (xl, y, 1 - c, z, 1 - xh) if c != xh else None,
    )
    ready, weights[0], pieces, moved = together(sliced[1], weights[0], pieces, moved)
    weights.append(lax.all_to_all(ready, "z", 0, 0, tiled=True))

    keep, *gives = project(place, weights[0], swap_core(weights[0]), pieces, ())
    gots = [swap_xh(give) for give in gives]
    hiddens = [activate(keep, gots)]

    weights[1], _ = together(weights[1], gots[0])
    mine = jnp.where(c == xh, down_weight, moved)

    both = together(weights[1], swap_core(weights[1]), hiddens[0])
    keep, give = project(place, *both[:2], pieces, ())
    got = swap_xh(give)
    hidden, _ = together(hiddens[0], give)
    first, (got, mine) = round_z(hidden, (got, mine), 1)
    theirs = swap_core(mine)
    second, _ = round_z(activate(keep, [got]), (first[3], first[-3]), -1)

    out = mix(place, (first, second), mine, theirs).reshape(16, tokens.shape[0], -1)
    got = lax.all_to_all(out, ("xh", "y", "xl"), 0, 0, tiled=True)
    return jnp.sum(got.astype(F32), 0)


def solution(mesh):
    split = Mesh(mesh.devices.reshape(SIZES), AXES)
    row, col = ("xl", "y", "c"), ("z", "xh")
    return jax.shard_map(
        shards,
        mesh=split,
        in_specs=(P(row, col), P(col, row), P(col, row), P(row, col)),
        out_specs=P(row, col),
        check_vma=False,
    )
```

```python
import functools
import itertools

import jax
import jax.numpy as jnp
from jax import lax
from jax.experimental import pallas as pl
from jax.experimental.pallas import tpu as pltpu
from jax.sharding import Mesh, PartitionSpec as P

AXES = ("xl", "y", "c", "z", "xh")
SIZES = (2, 4, 2, 8, 2)
FIRST = 160
TOGETHER = 2
F32, BF16 = jnp.float32, jnp.bfloat16
SCALARS = pl.BlockSpec(memory_space=pltpu.SMEM)
WHOLE = pl.BlockSpec(memory_space=pltpu.VMEM)


def send(value, move):
    flat = lambda at: sum(i * k for i, k in zip(at, (128, 32, 16, 2, 1)))
    pairs = []
    for at in itertools.product(*map(range, SIZES)):
        to = move(*at)
        if to is not None:
            pairs.append((flat(at), flat(tuple(i % n for i, n in zip(to, SIZES)))))
    return lax.ppermute(value, AXES, pairs)


def along_z(value, step):
    return send(value, lambda xl, y, c, z, xh: (xl, y, c, z + step, xh))


def along_y(value, step):
    return send(value, lambda xl, y, c, z, xh: (xl, y + step, c, z, xh))


def swap_xl(value):
    return send(value, lambda xl, y, c, z, xh: (1 - xl, y, c, z, xh))


def swap_xh(value):
    return send(value, lambda xl, y, c, z, xh: (xl, y, c, z, 1 - xh))


def swap_core(value):
    return send(value, lambda xl, y, c, z, xh: (xl, y, 1 - c, z, xh))


def together(*values):
    return lax.optimization_barrier(values)


def room(mib):
    return pltpu.CompilerParams(vmem_limit_bytes=mib << 20)


def cost(flops, *arrays):
    size = sum(a.size * a.dtype.itemsize for a in arrays)
    return pl.CostEstimate(flops=flops // 64, bytes_accessed=size // 64, transcendentals=0)


def regroup(place, parts):
    nz = SIZES[3]

    def body(place_ref, *rest):
        z = place_ref[3]
        for s, part_ref in enumerate(rest[:nz]):
            rest[nz][(z + nz - s) % nz] = part_ref[...]

    return pl.pallas_call(
        body,
        in_specs=[SCALARS] + [WHOLE] * nz,
        out_specs=WHOLE,
        out_shape=jax.ShapeDtypeStruct((nz, *parts[0].shape), BF16),
        cost_estimate=cost(0, *parts, *parts),
        name="regroup",
    )(place, *parts)


def slice_units(gate, up, nz):
    depth, width = gate.shape
    units = width // nz
    step = 256
    cuts = ((0, FIRST), (FIRST, units))

    def body(g_ref, u_ref, *o_refs):
        for w_ref, at in ((g_ref, 0), (u_ref, 1)):
            w = w_ref[...].T.reshape(nz, units, step)
            for (lo, hi), o_ref in zip(cuts, o_refs):
                o_ref[:, at * (hi - lo) : (at + 1) * (hi - lo)] = w[:, lo:hi]

    outs = [jax.ShapeDtypeStruct((nz, 2 * (hi - lo), depth), gate.dtype) for lo, hi in cuts]
    return pl.pallas_call(
        body,
        grid=(depth // step,),
        in_specs=[pl.BlockSpec((step, width), lambda k: (k, 0))] * 2,
        out_specs=[pl.BlockSpec((*o.shape[:2], step), lambda k: (0, 0, k)) for o in outs],
        out_shape=outs,
        cost_estimate=cost(0, gate, up, *outs),
        name="slice_units",
    )(gate, up)


def project(place, own, other, pieces, cuts):
    nz, units, depth = own.shape
    rows = pieces[0].shape[1]
    width = 8 * rows
    groups = nz // TOGETHER

    def body(place_ref, own_ref, other_ref, *rest):
        piece_refs, (keep_ref, *give_refs, t_ref, w_ref, acc_ref, sems) = rest[:8], rest[8:]
        xl, y = place_ref[0], place_ref[1]

        def copies(g):
            zs = pl.ds(g * TOGETHER, TOGETHER)
            pairs = [
                (own_ref.at[zs], w_ref.at[zs, pl.ds(0, units)]),
                (other_ref.at[zs], w_ref.at[zs, pl.ds(units, units)]),
            ]
            for n, piece_ref in enumerate(piece_refs):
                at = ((y + n // 2) % 4) * 2 + (xl + n % 2) % 2
                to = pl.multiple_of(at * rows, rows)
                pairs.append((piece_ref.at[zs], t_ref.at[zs, pl.ds(to, rows)]))
            return [pltpu.make_async_copy(*pair, sems.at[g, n]) for n, pair in enumerate(pairs)]

        @pl.loop(0, groups)
        def _(g):
            for copy in copies(g):
                copy.start()

        acc_ref[...] = jnp.zeros_like(acc_ref)

        @pl.loop(0, groups)
        def _(g):
            for copy in copies(g):
                copy.wait()
            for j in range(TOGETHER):
                acc_ref[...] += lax.dot_general(
                    w_ref[g * TOGETHER + j], t_ref[g * TOGETHER + j],
                    (((1,), (1,)), ((), ())), preferred_element_type=F32,
                )

        kept = pl.multiple_of(jnp.where(place_ref[2] == place_ref[4], 0, units), units)
        keep_ref[...] = acc_ref[pl.ds(kept, units)]
        for lo, hi, give_ref in zip((0, *cuts), (*cuts, units), give_refs):
            give_ref[...] = acc_ref[pl.ds(pl.multiple_of(units - kept + lo, 8), hi - lo)]

    outs = [
        jax.ShapeDtypeStruct((hi - lo, width), F32)
        for lo, hi in ((0, units), *zip((0, *cuts), (*cuts, units)))
    ]
    args = (own, other, *pieces)
    return pl.pallas_call(
        body,
        in_specs=[SCALARS] + [pl.BlockSpec(memory_space=pl.ANY)] * 10,
        out_specs=[WHOLE] * len(outs),
        out_shape=outs,
        scratch_shapes=[
            pltpu.VMEM((nz, width, depth), BF16),
            pltpu.VMEM((nz, 2 * units, depth), BF16),
            pltpu.VMEM((2 * units, width), F32),
            pltpu.SemaphoreType.DMA((groups, 10)),
        ],
        cost_estimate=cost(4 * nz * units * depth * width, *args),
        name="project",
    )(place, *args)


def activate(keep, gots):
    units, rows = keep.shape[0] // 2, keep.shape[1]

    def body(keep_ref, *rest):
        got_refs, (o_ref, sum_ref) = rest[:-2], rest[-2:]
        at = 0
        for got_ref in got_refs:
            here = slice(at, at + got_ref.shape[0])
            sum_ref[here] = keep_ref[here] + got_ref[...]
            at += got_ref.shape[0]
        gate, up = sum_ref[:units], sum_ref[units:]
        o_ref[...] = (gate / (1 + jnp.exp(-gate)) * up).astype(o_ref.dtype)

    return pl.pallas_call(
        body,
        in_specs=[WHOLE] * (1 + len(gots)),
        out_specs=WHOLE,
        out_shape=jax.ShapeDtypeStruct((units, rows), BF16),
        scratch_shapes=[pltpu.VMEM(keep.shape, F32)],
        cost_estimate=cost(0, keep, *gots),
        name="activate",
        compiler_params=room(8),
    )(keep, *gots)


def mix(place, rings, mine, theirs):
    nz = SIZES[3]
    sizes = [ring[0].shape[0] for ring in rings]
    units, rows = sum(sizes), rings[0][0].shape[1]
    width = mine.shape[1]
    order = (0, 1, 2, 3, 4, -3, -2, -1)
    parts = [ring[s] for ring in rings for s in order]

    def body(place_ref, mine_ref, theirs_ref, *rest):
        part_refs, (o_ref, h_ref) = list(rest[:-2]), rest[-2:]
        c, z = place_ref[2], place_ref[3]
        first = 0
        for size in sizes:
            for s in order:
                at = ((z - s + nz) % nz) * units + first
                h_ref[pl.ds(pl.multiple_of(at, 16), size)] = part_refs.pop(0)[...]
            first += size
        for side, w_ref in ((c, mine_ref), (1 - c, theirs_ref)):
            o_ref[side] = lax.dot_general(
                h_ref[...], w_ref[...], (((0,), (0,)), ((), ())), preferred_element_type=F32
            ).astype(o_ref.dtype)

    return pl.pallas_call(
        body,
        in_specs=[SCALARS] + [WHOLE] * (2 + len(parts)),
        out_specs=WHOLE,
        out_shape=jax.ShapeDtypeStruct((2, rows, width), BF16),
        scratch_shapes=[pltpu.VMEM((nz * units, rows), BF16)],
        cost_estimate=cost(4 * nz * units * rows * width, mine, theirs, *parts),
        name="mix",
        compiler_params=room(24),
    )(place, mine, theirs, *parts)


def round_z(hidden, other, way):
    ring = {0: hidden}
    up = down = hidden
    for at in (1, 2, 3):
        up, down = along_z(up, 1), along_z(down, -1)
        if at == 2:
            up, down, other = together(up, down, other)
        ring.update({at: up, -at: down})
    ring[4] = along_z(up if way > 0 else down, way)
    return ring, other


def shards(tokens, gate_weight, up_weight, down_weight):
    xl, y, c, z, xh = (lax.axis_index(a) for a in AXES)
    place = jnp.stack([xl, y, c, z, xh]).astype(jnp.int32)
    nz = SIZES[3]

    around = {0: tokens}
    for s in (1, -1, 2, -2, 4):
        around[s] = along_z(tokens, s)
    around[3], around[-3] = along_z(around[2], 1), along_z(around[-2], -1)
    sliced = slice_units(gate_weight, up_weight, nz)
    near = regroup(place, [around[s] for s in (0, 1, 2, 3, 4, -3, -2, -1)])
    ready, near = together(sliced[0], near)
    weights = [lax.all_to_all(ready, "z", 0, 0, tiled=True)]

    far = swap_xl(near)
    near_before, near_after = along_y(near, 1), along_y(near, -1)
    far, near_before, near_after = together(far, near_before, near_after)
    far_before, far_after = along_y(far, 1), along_y(far, -1)
    near_across, far_across = along_y(near_before, 1), along_y(far_after, -1)
    pieces = (near, far, near_after, far_after, near_across, far_across, near_before, far_before)
    down_weight, _ = together(down_weight, far)
    moved = send(
        down_weight,
        lambda xl, y, c, z, xh: (xl, y, 1 - c, z, 1 - xh) if c != xh else None,
    )
    ready, weights[0], pieces, moved = together(sliced[1], weights[0], pieces, moved)
    weights.append(lax.all_to_all(ready, "z", 0, 0, tiled=True))

    keep, *gives = project(place, weights[0], swap_core(weights[0]), pieces, ())
    gots = [swap_xh(give) for give in gives]
    hiddens = [activate(keep, gots)]

    weights[1], _ = together(weights[1], gots[0])
    mine = jnp.where(c == xh, down_weight, moved)

    both = together(weights[1], swap_core(weights[1]), hiddens[0])
    keep, give = project(place, *both[:2], pieces, ())
    got = swap_xh(give)
    hidden, _ = together(hiddens[0], give)
    first, (got, mine) = round_z(hidden, (got, mine), 1)
    theirs = swap_core(mine)
    second, _ = round_z(activate(keep, [got]), (first[3], first[-3]), -1)

    out = mix(place, (first, second), mine, theirs).reshape(16, tokens.shape[0], -1)
    got = lax.all_to_all(out, ("xh", "y", "xl"), 0, 0, tiled=True)
    return jnp.sum(got.astype(F32), 0)


def solution(mesh):
    split = Mesh(mesh.devices.reshape(SIZES), AXES)
    row, col = ("xl", "y", "c"), ("z", "xh")
    return jax.shard_map(
        shards,
        mesh=split,
        in_specs=(P(row, col), P(col, row), P(col, row), P(row, col)),
        out_specs=P(row, col),
        check_vma=False,
    )
```

```python
import functools
import itertools

import jax
import jax.numpy as jnp
from jax import lax
from jax.experimental import pallas as pl
from jax.experimental.pallas import tpu as pltpu
from jax.sharding import Mesh, PartitionSpec as P

AXES = ("xl", "y", "c", "z", "xh")
SIZES = (2, 4, 2, 8, 2)
FIRST = 144
TOGETHER = 2
F32, BF16 = jnp.float32, jnp.bfloat16
SCALARS = pl.BlockSpec(memory_space=pltpu.SMEM)
WHOLE = pl.BlockSpec(memory_space=pltpu.VMEM)


def send(value, move):
    flat = lambda at: sum(i * k for i, k in zip(at, (128, 32, 16, 2, 1)))
    pairs = []
    for at in itertools.product(*map(range, SIZES)):
        to = move(*at)
        if to is not None:
            pairs.append((flat(at), flat(tuple(i % n for i, n in zip(to, SIZES)))))
    return lax.ppermute(value, AXES, pairs)


def along_z(value, step):
    return send(value, lambda xl, y, c, z, xh: (xl, y, c, z + step, xh))


def along_y(value, step):
    return send(value, lambda xl, y, c, z, xh: (xl, y + step, c, z, xh))


def swap_xl(value):
    return send(value, lambda xl, y, c, z, xh: (1 - xl, y, c, z, xh))


def swap_xh(value):
    return send(value, lambda xl, y, c, z, xh: (xl, y, c, z, 1 - xh))


def swap_core(value):
    return send(value, lambda xl, y, c, z, xh: (xl, y, 1 - c, z, xh))


def together(*values):
    return lax.optimization_barrier(values)


def room(mib):
    return pltpu.CompilerParams(vmem_limit_bytes=mib << 20)


def cost(flops, *arrays):
    size = sum(a.size * a.dtype.itemsize for a in arrays)
    return pl.CostEstimate(flops=flops // 64, bytes_accessed=size // 64, transcendentals=0)


def regroup(place, parts):
    nz = SIZES[3]

    def body(place_ref, *rest):
        z = place_ref[3]
        for s, part_ref in enumerate(rest[:nz]):
            rest[nz][(z + nz - s) % nz] = part_ref[...]

    return pl.pallas_call(
        body,
        in_specs=[SCALARS] + [WHOLE] * nz,
        out_specs=WHOLE,
        out_shape=jax.ShapeDtypeStruct((nz, *parts[0].shape), BF16),
        cost_estimate=cost(0, *parts, *parts),
        name="regroup",
    )(place, *parts)


def slice_units(gate, up, nz):
    depth, width = gate.shape
    units = width // nz
    step = 256
    cuts = ((0, FIRST), (FIRST, units))

    def body(g_ref, u_ref, *o_refs):
        for w_ref, at in ((g_ref, 0), (u_ref, 1)):
            w = w_ref[...].T.reshape(nz, units, step)
            for (lo, hi), o_ref in zip(cuts, o_refs):
                o_ref[:, at * (hi - lo) : (at + 1) * (hi - lo)] = w[:, lo:hi]

    outs = [jax.ShapeDtypeStruct((nz, 2 * (hi - lo), depth), gate.dtype) for lo, hi in cuts]
    return pl.pallas_call(
        body,
        grid=(depth // step,),
        in_specs=[pl.BlockSpec((step, width), lambda k: (k, 0))] * 2,
        out_specs=[pl.BlockSpec((*o.shape[:2], step), lambda k: (0, 0, k)) for o in outs],
        out_shape=outs,
        cost_estimate=cost(0, gate, up, *outs),
        name="slice_units",
    )(gate, up)


def project(place, own, other, pieces, cuts):
    nz, units, depth = own.shape
    rows = pieces[0].shape[1]
    width = 8 * rows
    groups = nz // TOGETHER

    def body(place_ref, own_ref, other_ref, *rest):
        piece_refs, (keep_ref, *give_refs, t_ref, w_ref, acc_ref, sems) = rest[:8], rest[8:]
        xl, y = place_ref[0], place_ref[1]

        def copies(g):
            zs = pl.ds(g * TOGETHER, TOGETHER)
            pairs = [
                (own_ref.at[zs], w_ref.at[zs, pl.ds(0, units)]),
                (other_ref.at[zs], w_ref.at[zs, pl.ds(units, units)]),
            ]
            for n, piece_ref in enumerate(piece_refs):
                at = ((y + n // 2) % 4) * 2 + (xl + n % 2) % 2
                to = pl.multiple_of(at * rows, rows)
                pairs.append((piece_ref.at[zs], t_ref.at[zs, pl.ds(to, rows)]))
            return [pltpu.make_async_copy(*pair, sems.at[g, n]) for n, pair in enumerate(pairs)]

        @pl.loop(0, groups)
        def _(g):
            for copy in copies(g):
                copy.start()

        acc_ref[...] = jnp.zeros_like(acc_ref)

        @pl.loop(0, groups)
        def _(g):
            for copy in copies(g):
                copy.wait()
            for j in range(TOGETHER):
                acc_ref[...] += lax.dot_general(
                    w_ref[g * TOGETHER + j], t_ref[g * TOGETHER + j],
                    (((1,), (1,)), ((), ())), preferred_element_type=F32,
                )

        kept = pl.multiple_of(jnp.where(place_ref[2] == place_ref[4], 0, units), units)
        keep_ref[...] = acc_ref[pl.ds(kept, units)]
        for lo, hi, give_ref in zip((0, *cuts), (*cuts, units), give_refs):
            give_ref[...] = acc_ref[pl.ds(pl.multiple_of(units - kept + lo, 8), hi - lo)]

    outs = [
        jax.ShapeDtypeStruct((hi - lo, width), F32)
        for lo, hi in ((0, units), *zip((0, *cuts), (*cuts, units)))
    ]
    args = (own, other, *pieces)
    return pl.pallas_call(
        body,
        in_specs=[SCALARS] + [pl.BlockSpec(memory_space=pl.ANY)] * 10,
        out_specs=[WHOLE] * len(outs),
        out_shape=outs,
        scratch_shapes=[
            pltpu.VMEM((nz, width, depth), BF16),
            pltpu.VMEM((nz, 2 * units, depth), BF16),
            pltpu.VMEM((2 * units, width), F32),
            pltpu.SemaphoreType.DMA((groups, 10)),
        ],
        cost_estimate=cost(4 * nz * units * depth * width, *args),
        name="project",
    )(place, *args)


def activate(keep, gots):
    units, rows = keep.shape[0] // 2, keep.shape[1]

    def body(keep_ref, *rest):
        got_refs, (o_ref, sum_ref) = rest[:-2], rest[-2:]
        at = 0
        for got_ref in got_refs:
            here = slice(at, at + got_ref.shape[0])
            sum_ref[here] = keep_ref[here] + got_ref[...]
            at += got_ref.shape[0]
        gate, up = sum_ref[:units], sum_ref[units:]
        o_ref[...] = (gate / (1 + jnp.exp(-gate)) * up).astype(o_ref.dtype)

    return pl.pallas_call(
        body,
        in_specs=[WHOLE] * (1 + len(gots)),
        out_specs=WHOLE,
        out_shape=jax.ShapeDtypeStruct((units, rows), BF16),
        scratch_shapes=[pltpu.VMEM(keep.shape, F32)],
        cost_estimate=cost(0, keep, *gots),
        name="activate",
        compiler_params=room(8),
    )(keep, *gots)


def mix(place, rings, mine, theirs):
    nz = SIZES[3]
    sizes = [ring[0].shape[0] for ring in rings]
    units, rows = sum(sizes), rings[0][0].shape[1]
    width = mine.shape[1]
    order = (0, 1, 2, 3, 4, -3, -2, -1)
    parts = [ring[s] for ring in rings for s in order]

    def body(place_ref, mine_ref, theirs_ref, *rest):
        part_refs, (o_ref, h_ref) = list(rest[:-2]), rest[-2:]
        c, z = place_ref[2], place_ref[3]
        first = 0
        for size in sizes:
            for s in order:
                at = ((z - s + nz) % nz) * units + first
                h_ref[pl.ds(pl.multiple_of(at, 16), size)] = part_refs.pop(0)[...]
            first += size
        for side, w_ref in ((c, mine_ref), (1 - c, theirs_ref)):
            o_ref[side] = lax.dot_general(
                h_ref[...], w_ref[...], (((0,), (0,)), ((), ())), preferred_element_type=F32
            ).astype(o_ref.dtype)

    return pl.pallas_call(
        body,
        in_specs=[SCALARS] + [WHOLE] * (2 + len(parts)),
        out_specs=WHOLE,
        out_shape=jax.ShapeDtypeStruct((2, rows, width), BF16),
        scratch_shapes=[pltpu.VMEM((nz * units, rows), BF16)],
        cost_estimate=cost(4 * nz * units * rows * width, mine, theirs, *parts),
        name="mix",
        compiler_params=room(24),
    )(place, mine, theirs, *parts)


def round_z(hidden, other, way):
    ring = {0: hidden}
    up = down = hidden
    for at in (1, 2, 3):
        up, down = along_z(up, 1), along_z(down, -1)
        if at == 2:
            up, down, other = together(up, down, other)
        ring.update({at: up, -at: down})
    ring[4] = along_z(up if way > 0 else down, way)
    return ring, other


def shards(tokens, gate_weight, up_weight, down_weight):
    xl, y, c, z, xh = (lax.axis_index(a) for a in AXES)
    place = jnp.stack([xl, y, c, z, xh]).astype(jnp.int32)
    nz = SIZES[3]

    around = {0: tokens}
    for s in (4, 3, -3, 2, -2, 1, -1):
        around[s] = along_z(tokens, s)
    sliced = slice_units(gate_weight, up_weight, nz)
    near = regroup(place, [around[s] for s in (0, 1, 2, 3, 4, -3, -2, -1)])
    ready, near = together(sliced[0], near)
    weights = [lax.all_to_all(ready, "z", 0, 0, tiled=True)]

    far = swap_xl(near)
    near_before, near_after = along_y(near, 1), along_y(near, -1)
    far, near_before, near_after = together(far, near_before, near_after)
    far_before, far_after = along_y(far, 1), along_y(far, -1)
    near_across, far_across = along_y(near_before, 1), along_y(far_after, -1)
    pieces = (near, far, near_after, far_after, near_across, far_across, near_before, far_before)
    down_weight, _ = together(down_weight, far)
    moved = send(
        down_weight,
        lambda xl, y, c, z, xh: (xl, y, 1 - c, z, 1 - xh) if c != xh else None,
    )
    ready, weights[0], pieces, moved = together(sliced[1], weights[0], pieces, moved)
    weights.append(lax.all_to_all(ready, "z", 0, 0, tiled=True))

    keep, *gives = project(place, weights[0], swap_core(weights[0]), pieces, ())
    gots = [swap_xh(give) for give in gives]
    hiddens = [activate(keep, gots)]

    weights[1], _ = together(weights[1], gots[0])
    mine = jnp.where(c == xh, down_weight, moved)

    both = together(weights[1], swap_core(weights[1]), hiddens[0])
    keep, give = project(place, *both[:2], pieces, ())
    got = swap_xh(give)
    hidden, _ = together(hiddens[0], give)
    first, (got, mine) = round_z(hidden, (got, mine), 1)
    theirs = swap_core(mine)
    second, _ = round_z(activate(keep, [got]), (first[3], first[-3]), -1)

    out = mix(place, (first, second), mine, theirs).reshape(16, tokens.shape[0], -1)
    got = lax.all_to_all(out, ("xh", "y", "xl"), 0, 0, tiled=True)
    return jnp.sum(got.astype(F32), 0)


def solution(mesh):
    split = Mesh(mesh.devices.reshape(SIZES), AXES)
    row, col = ("xl", "y", "c"), ("z", "xh")
    return jax.shard_map(
        shards,
        mesh=split,
        in_specs=(P(row, col), P(col, row), P(col, row), P(row, col)),
        out_specs=P(row, col),
        check_vma=False,
    )
```

```python
import functools
import itertools

import jax
import jax.numpy as jnp
from jax import lax
from jax.experimental import pallas as pl
from jax.experimental.pallas import tpu as pltpu
from jax.sharding import Mesh, PartitionSpec as P

AXES = ("xl", "y", "c", "z", "xh")
SIZES = (2, 4, 2, 8, 2)
FIRST = 144
TOGETHER = 2
F32, BF16 = jnp.float32, jnp.bfloat16
SCALARS = pl.BlockSpec(memory_space=pltpu.SMEM)
WHOLE = pl.BlockSpec(memory_space=pltpu.VMEM)


def send(value, move):
    flat = lambda at: sum(i * k for i, k in zip(at, (128, 32, 16, 2, 1)))
    pairs = []
    for at in itertools.product(*map(range, SIZES)):
        to = move(*at)
        if to is not None:
            pairs.append((flat(at), flat(tuple(i % n for i, n in zip(to, SIZES)))))
    return lax.ppermute(value, AXES, pairs)


def along_z(value, step):
    return send(value, lambda xl, y, c, z, xh: (xl, y, c, z + step, xh))


def along_y(value, step):
    return send(value, lambda xl, y, c, z, xh: (xl, y + step, c, z, xh))


def swap_xl(value):
    return send(value, lambda xl, y, c, z, xh: (1 - xl, y, c, z, xh))


def swap_xh(value):
    return send(value, lambda xl, y, c, z, xh: (xl, y, c, z, 1 - xh))


def swap_core(value):
    return send(value, lambda xl, y, c, z, xh: (xl, y, 1 - c, z, xh))


def together(*values):
    return lax.optimization_barrier(values)


def room(mib):
    return pltpu.CompilerParams(vmem_limit_bytes=mib << 20)


def cost(flops, *arrays):
    size = sum(a.size * a.dtype.itemsize for a in arrays)
    return pl.CostEstimate(flops=flops // 64, bytes_accessed=size // 64, transcendentals=0)


def regroup(place, parts):
    nz = SIZES[3]

    def body(place_ref, *rest):
        z = place_ref[3]
        for s, part_ref in enumerate(rest[:nz]):
            rest[nz][(z + nz - s) % nz] = part_ref[...]

    return pl.pallas_call(
        body,
        in_specs=[SCALARS] + [WHOLE] * nz,
        out_specs=WHOLE,
        out_shape=jax.ShapeDtypeStruct((nz, *parts[0].shape), BF16),
        cost_estimate=cost(0, *parts, *parts),
        name="regroup",
    )(place, *parts)


def slice_units(gate, up, nz):
    depth, width = gate.shape
    units = width // nz
    step = 256
    cuts = ((0, FIRST), (FIRST, units))

    def body(g_ref, u_ref, *o_refs):
        for w_ref, at in ((g_ref, 0), (u_ref, 1)):
            w = w_ref[...].T.reshape(nz, units, step)
            for (lo, hi), o_ref in zip(cuts, o_refs):
                o_ref[:, at * (hi - lo) : (at + 1) * (hi - lo)] = w[:, lo:hi]

    outs = [jax.ShapeDtypeStruct((nz, 2 * (hi - lo), depth), gate.dtype) for lo, hi in cuts]
    return pl.pallas_call(
        body,
        grid=(depth // step,),
        in_specs=[pl.BlockSpec((step, width), lambda k: (k, 0))] * 2,
        out_specs=[pl.BlockSpec((*o.shape[:2], step), lambda k: (0, 0, k)) for o in outs],
        out_shape=outs,
        cost_estimate=cost(0, gate, up, *outs),
        name="slice_units",
    )(gate, up)


def project(place, own, other, pieces, cuts):
    nz, units, depth = own.shape
    rows = pieces[0].shape[1]
    width = 8 * rows
    groups = nz // TOGETHER

    def body(place_ref, own_ref, other_ref, *rest):
        piece_refs, (keep_ref, *give_refs, t_ref, w_ref, acc_ref, sems) = rest[:8], rest[8:]
        xl, y = place_ref[0], place_ref[1]

        def copies(g):
            zs = pl.ds(g * TOGETHER, TOGETHER)
            pairs = [
                (own_ref.at[zs], w_ref.at[zs, pl.ds(0, units)]),
                (other_ref.at[zs], w_ref.at[zs, pl.ds(units, units)]),
            ]
            for n, piece_ref in enumerate(piece_refs):
                at = ((y + n // 2) % 4) * 2 + (xl + n % 2) % 2
                to = pl.multiple_of(at * rows, rows)
                pairs.append((piece_ref.at[zs], t_ref.at[zs, pl.ds(to, rows)]))
            return [pltpu.make_async_copy(*pair, sems.at[g, n]) for n, pair in enumerate(pairs)]

        @pl.loop(0, groups)
        def _(g):
            for copy in copies(g):
                copy.start()

        acc_ref[...] = jnp.zeros_like(acc_ref)

        @pl.loop(0, groups)
        def _(g):
            for copy in copies(g):
                copy.wait()
            for j in range(TOGETHER):
                acc_ref[...] += lax.dot_general(
                    w_ref[g * TOGETHER + j], t_ref[g * TOGETHER + j],
                    (((1,), (1,)), ((), ())), preferred_element_type=F32,
                )

        kept = pl.multiple_of(jnp.where(place_ref[2] == place_ref[4], 0, units), units)
        keep_ref[...] = acc_ref[pl.ds(kept, units)]
        for lo, hi, give_ref in zip((0, *cuts), (*cuts, units), give_refs):
            give_ref[...] = acc_ref[pl.ds(pl.multiple_of(units - kept + lo, 8), hi - lo)]

    outs = [
        jax.ShapeDtypeStruct((hi - lo, width), F32)
        for lo, hi in ((0, units), *zip((0, *cuts), (*cuts, units)))
    ]
    args = (own, other, *pieces)
    return pl.pallas_call(
        body,
        in_specs=[SCALARS] + [pl.BlockSpec(memory_space=pl.ANY)] * 10,
        out_specs=[WHOLE] * len(outs),
        out_shape=outs,
        scratch_shapes=[
            pltpu.VMEM((nz, width, depth), BF16),
            pltpu.VMEM((nz, 2 * units, depth), BF16),
            pltpu.VMEM((2 * units, width), F32),
            pltpu.SemaphoreType.DMA((groups, 10)),
        ],
        cost_estimate=cost(4 * nz * units * depth * width, *args),
        name="project",
    )(place, *args)


def activate(keep, gots):
    units, rows = keep.shape[0] // 2, keep.shape[1]

    def body(keep_ref, *rest):
        got_refs, (o_ref, sum_ref) = rest[:-2], rest[-2:]
        at = 0
        for got_ref in got_refs:
            here = slice(at, at + got_ref.shape[0])
            sum_ref[here] = keep_ref[here] + got_ref[...]
            at += got_ref.shape[0]
        gate, up = sum_ref[:units], sum_ref[units:]
        o_ref[...] = (gate / (1 + jnp.exp(-gate)) * up).astype(o_ref.dtype)

    return pl.pallas_call(
        body,
        in_specs=[WHOLE] * (1 + len(gots)),
        out_specs=WHOLE,
        out_shape=jax.ShapeDtypeStruct((units, rows), BF16),
        scratch_shapes=[pltpu.VMEM(keep.shape, F32)],
        cost_estimate=cost(0, keep, *gots),
        name="activate",
        compiler_params=room(8),
    )(keep, *gots)


def mix(place, rings, mine, theirs):
    nz = SIZES[3]
    sizes = [ring[0].shape[0] for ring in rings]
    units, rows = sum(sizes), rings[0][0].shape[1]
    width = mine.shape[1]
    order = (0, 1, 2, 3, 4, -3, -2, -1)
    parts = [ring[s] for ring in rings for s in order]

    def body(place_ref, mine_ref, theirs_ref, *rest):
        part_refs, (o_ref, h_ref) = list(rest[:-2]), rest[-2:]
        c, z = place_ref[2], place_ref[3]
        first = 0
        for size in sizes:
            for s in order:
                at = ((z - s + nz) % nz) * units + first
                h_ref[pl.ds(pl.multiple_of(at, 16), size)] = part_refs.pop(0)[...]
            first += size
        for side, w_ref in ((c, mine_ref), (1 - c, theirs_ref)):
            o_ref[side] = lax.dot_general(
                h_ref[...], w_ref[...], (((0,), (0,)), ((), ())), preferred_element_type=F32
            ).astype(o_ref.dtype)

    return pl.pallas_call(
        body,
        in_specs=[SCALARS] + [WHOLE] * (2 + len(parts)),
        out_specs=WHOLE,
        out_shape=jax.ShapeDtypeStruct((2, rows, width), BF16),
        scratch_shapes=[pltpu.VMEM((nz * units, rows), BF16)],
        cost_estimate=cost(4 * nz * units * rows * width, mine, theirs, *parts),
        name="mix",
        compiler_params=room(24),
    )(place, mine, theirs, *parts)


def round_z(hidden, other, way):
    ring = {0: hidden}
    up = down = hidden
    for at in (1, 2, 3):
        up, down = along_z(up, 1), along_z(down, -1)
        if at == 2:
            up, down, other = together(up, down, other)
        ring.update({at: up, -at: down})
    ring[4] = along_z(up if way > 0 else down, way)
    return ring, other


def shards(tokens, gate_weight, up_weight, down_weight):
    xl, y, c, z, xh = (lax.axis_index(a) for a in AXES)
    place = jnp.stack([xl, y, c, z, xh]).astype(jnp.int32)
    nz = SIZES[3]

    around = {0: tokens}
    for s in (1, -1, 2, -2, 4):
        around[s] = along_z(tokens, s)
    around[3], around[-3] = along_z(around[2], 1), along_z(around[-2], -1)
    sliced = slice_units(gate_weight, up_weight, nz)
    near = regroup(place, [around[s] for s in (0, 1, 2, 3, 4, -3, -2, -1)])
    ready, near = together(sliced[0], near)
    weights = [lax.all_to_all(ready, "z", 0, 0, tiled=True)]

    far = swap_xl(near)
    near_before, near_after = along_y(near, 1), along_y(near, -1)
    far, near_before, near_after = together(far, near_before, near_after)
    far_before, far_after = along_y(far, 1), along_y(far, -1)
    near_across, far_across = along_y(near_before, 1), along_y(far_after, -1)
    pieces = (near, far, near_after, far_after, near_across, far_across, near_before, far_before)
    down_weight, _ = together(down_weight, far)
    moved = send(
        down_weight,
        lambda xl, y, c, z, xh: (xl, y, 1 - c, z, 1 - xh) if c != xh else None,
    )
    ready, weights[0], pieces, moved = together(sliced[1], weights[0], pieces, moved)
    weights.append(lax.all_to_all(ready, "z", 0, 0, tiled=True))

    keep, *gives = project(place, weights[0], swap_core(weights[0]), pieces, ())
    gots = [swap_xh(give) for give in gives]
    hiddens = [activate(keep, gots)]

    weights[1], _ = together(weights[1], hiddens[0])
    mine = jnp.where(c == xh, down_weight, moved)

    both = together(weights[1], swap_core(weights[1]), hiddens[0])
    keep, give = project(place, *both[:2], pieces, ())
    got = swap_xh(give)
    hidden, _ = together(hiddens[0], give)
    first, (got, mine) = round_z(hidden, (got, mine), 1)
    theirs = swap_core(mine)
    second, _ = round_z(activate(keep, [got]), (first[3], first[-3]), -1)

    out = mix(place, (first, second), mine, theirs).reshape(16, tokens.shape[0], -1)
    got = lax.all_to_all(out, ("xh", "y", "xl"), 0, 0, tiled=True)
    return jnp.sum(got.astype(F32), 0)


def solution(mesh):
    split = Mesh(mesh.devices.reshape(SIZES), AXES)
    row, col = ("xl", "y", "c"), ("z", "xh")
    return jax.shard_map(
        shards,
        mesh=split,
        in_specs=(P(row, col), P(col, row), P(col, row), P(row, col)),
        out_specs=P(row, col),
        check_vma=False,
    )
```
